32 devices in a mesh: prow: 4 (over y, core), pcol: 8 (over z, x).
Axes of the slice: x: 2, y: 2, z: 4, core: 2. Of those that a mesh axis runs over, the one named last changes fastest.
Arguments:
- right_side: float32 [8, 256, 128], P(None, 'prow'), may hold values from -6 to 6
- lower_prev: float32 [8, 256, 129024], P(None, 'prow', 'pcol'), may hold values from -0.015625 to 0.015625
- solved_prev: float32 [129024, 128], P('pcol'), may hold values from -6 to 6
- lower_window: float32 [8, 256, 2048], P(None, 'prow', 'pcol'), may hold values from -0.1875 to 0.1875
- inverse_diag: float32 [8, 256, 256], P(None, 'prow'), may hold values from -0.25 to 1.4, as said below
Outputs:
- solution: float32 [8, 256, 128], P(None, 'prow')
The draws below stay inside these ranges and needn't reach their ends.
Inputs may be any that keep to these rules, and one draw needn't show every extreme that they name: `inverse_diag`: each block is lower triangular: zero above its diagonal, with diagonal entries of 0.7 to 1.4.
All inputs are finite; a program needn't handle non-finite values.
Results may differ from the reference program's by a relative error of at most 0.00011.
Values sent between devices are 32-bit elements; how exact they have to be, the bound alone decides.
No kernel may reach another device: no remote copies, remote signals or barrier semaphores. Data moves between devices by JAX's collectives and lax.ppermute only.
A program may use at most 128 MiB of HBM per device.

```python
import jax
import jax.numpy as jnp
from jax import lax

N = 131072
NB = 256
WB = 8
RHS = 128
W = 2048
N_PREV = 129024


def draw_inverse_diag(key, part):
    diag_key = jax.random.fold_in(key, 11)
    off_key = jax.random.fold_in(key, 23)
    row_ids = jnp.arange(NB)[:, None]
    col_ids = jnp.arange(NB)[None, :]
    below = (row_ids > col_ids).astype(jnp.float32)
    on_diag = (row_ids == col_ids).astype(jnp.float32)
    scale_off = 0.5 * NB ** (-0.5)
    diag_vals = jnp.exp(jax.random.uniform(diag_key, (WB, NB, NB), jnp.float32, jnp.log(0.7), jnp.log(1.4)))
    off_vals = jnp.clip(jax.random.normal(off_key, (WB, NB, NB), jnp.float32), -4.0, 4.0) * scale_off
    return on_diag * diag_vals + below * off_vals


def shard_levels(stream_key, shape, split, smallest, high):
    level = 1.0
    for position, parts in split:
        heights = jax.random.uniform(jax.random.fold_in(jax.random.fold_in(stream_key, 6), position), (parts,), jnp.float32, smallest / len(split), high / len(split))
        level = level * jnp.repeat(jnp.exp(heights), shape[position] // parts).reshape((-1,) + (1,) * (len(shape) - 1 - position))
    return level


def scatter_about(own_key, extent, deviation, bound, pieces=(), dtype=jnp.bfloat16):
    drawn = deviation * jax.random.normal(own_key, extent, jnp.float32)
    if pieces:
        drawn = drawn * shard_levels(own_key, extent, pieces, -0.22, 0.18)
    return jnp.clip(drawn, -bound, bound).astype(dtype)


def setup_inputs(seed: int = 0) -> dict:
    keys = jax.random.split(jax.random.key(seed), 6)
    right_side = scatter_about(keys[0], (WB, NB, RHS), 1.0, 6.0, ((1, 4),), jnp.float32)
    lower_prev = scatter_about(keys[1], (WB, NB, N_PREV), N ** -0.5, 0.015625, ((1, 4), (2, 8)), jnp.float32)
    solved_prev = scatter_about(keys[2], (N_PREV, RHS), 1.0, 6.0, ((0, 8),), jnp.float32)
    lower_window = scatter_about(keys[3], (WB, NB, W), (4 * NB) ** -0.5, 0.1875, ((1, 4), (2, 8)), jnp.float32)
    inverse_diag = draw_inverse_diag(jax.random.fold_in(keys[5], 71), 0)
    return dict(right_side=right_side, lower_prev=lower_prev, solved_prev=solved_prev, lower_window=lower_window, inverse_diag=inverse_diag)


def reference(right_side, lower_prev, solved_prev, lower_window, inverse_diag):
    highest = lax.Precision.HIGHEST
    solved = jnp.zeros((WB * NB, RHS), jnp.float32)
    results = []
    for row_block in range(WB):
        earlier = jnp.dot(lower_prev[row_block], solved_prev, precision=highest, preferred_element_type=jnp.float32)
        window_term = jnp.dot(lower_window[row_block], solved, precision=highest, preferred_element_type=jnp.float32)
        residual = right_side[row_block] - (earlier + window_term)
        own_rows = jnp.dot(inverse_diag[row_block], residual, precision=highest, preferred_element_type=jnp.float32)
        results.append(own_rows)
        solved = lax.dynamic_update_slice_in_dim(solved, own_rows, row_block * NB, 0)
    return jnp.stack(results)
```

```python
import functools

import jax
import jax.numpy as jnp
from jax import lax
from jax.experimental import pallas as pl
from jax.experimental.pallas import tpu as pltpu
from jax.sharding import Mesh, PartitionSpec as P

F32 = jnp.float32
BF16 = jnp.bfloat16
EVERY = ("z", "y", "core", "x")
SWAP = [(0, 1), (1, 0)]
PLANES = 4
RHS_PART = 16
SUPER = 512
VMEM_LIMIT = 56 << 20


def halves(value):
    high = value.astype(BF16)
    low = (value - high.astype(F32)).astype(BF16)
    return high, low


def dot_f32(a, b):
    return jnp.dot(a, b, preferred_element_type=F32)


def dot_rows(a, b):
    return lax.dot_general(a, b, (((1,), (1,)), ((), ())), preferred_element_type=F32)


def add_products(factor_ref, solved_ref, total):
    factor_high, factor_low = halves(factor_ref[...])
    solved_both = jnp.concatenate(halves(solved_ref[...]), axis=1)
    total[...] += dot_f32(factor_high, solved_both) + dot_f32(factor_low, solved_both)


def earlier_first(factor_ref, solved_ref, total_ref):
    @pl.when(pl.program_id(0) == 0)
    def _():
        total_ref[...] = jnp.zeros_like(total_ref)

    add_products(factor_ref, solved_ref, total_ref)


def earlier_last(first_ref, factor_ref, solved_ref, total_in, right_ref, out_ref, total):
    step = pl.program_id(0)

    @pl.when(step == 0)
    def _():
        total[...] = total_in[...]

    add_products(factor_ref, solved_ref, total)

    @pl.when(step == pl.num_programs(0) - 1)
    def _():
        keep = first_ref[0] == 0
        width = right_ref.shape[1]
        for part in range(PLANES):
            rows = slice(part * 128, part * 128 + 128)
            earlier = total[rows, :width] + total[rows, width:]
            right = jnp.where(keep, right_ref[rows, :], 0.0)
            out_ref[part] = (right - earlier).T


def earlier_sums(first, factor, solved, right, tile, head):
    rows, depth = factor.shape
    columns = solved.shape[1]
    steps = depth // tile

    def cost(count):
        return pl.CostEstimate(
            flops=8 * rows * columns * tile * count,
            bytes_accessed=4 * (rows + columns) * tile * count,
            transcendentals=0,
        )

    total = pl.pallas_call(
        earlier_first,
        out_shape=jax.ShapeDtypeStruct((rows, 2 * columns), F32),
        grid=(head,),
        in_specs=[
            pl.BlockSpec((rows, tile), lambda k: (0, k)),
            pl.BlockSpec((tile, columns), lambda k: (k, 0)),
        ],
        out_specs=pl.BlockSpec((rows, 2 * columns), lambda k: (0, 0)),
        compiler_params=pltpu.CompilerParams(vmem_limit_bytes=VMEM_LIMIT),
        cost_estimate=cost(head),
        name="earlier_first",
    )(factor, solved)

    def finish(total):
        return pl.pallas_call(
            earlier_last,
            out_shape=jax.ShapeDtypeStruct((PLANES, columns, 128), F32),
            grid=(steps - head,),
            in_specs=[
                pl.BlockSpec(memory_space=pltpu.SMEM),
                pl.BlockSpec((rows, tile), lambda k: (0, k + head)),
                pl.BlockSpec((tile, columns), lambda k: (k + head, 0)),
                pl.BlockSpec((rows, 2 * columns), lambda k: (0, 0)),
                pl.BlockSpec((rows, columns), lambda k: (0, 0)),
            ],
            out_specs=pl.BlockSpec((PLANES, columns, 128), lambda k: (0, 0, 0)),
            scratch_shapes=[pltpu.VMEM((rows, 2 * columns), F32)],
            compiler_params=pltpu.CompilerParams(vmem_limit_bytes=VMEM_LIMIT),
            cost_estimate=cost(steps - head),
            name="earlier_last",
        )(first, factor, solved, total, right)

    return total, finish


def arrange(place_ref, *refs):
    pieces, out_ref = refs[:-1], refs[-1]
    y, core, x = place_ref[0], place_ref[1], place_ref[2]
    for index, (dy, dx, start, count) in enumerate(PIECES):
        for other in range(2):
            piece = pieces[2 * index + other]
            row_part = 2 * (y + dy - 2 * y * dy) + (core + other - 2 * core * other)
            column = x + dx - 2 * x * dx
            for j in range(count):
                block = start + j
                apart, b = block // 2, block % 2
                if apart == 0:
                    b = column if block == 0 else 1 - column
                row = pl.multiple_of(b * 256 + row_part * 64, 64)
                high, low = halves(piece[j])
                where = (pl.ds(row, 64), pl.ds(pl.multiple_of(column * 256, 256), 256))
                out_ref[(apart, 0) + where] = high
                out_ref[(apart, 1) + where] = low


PIECES = ((0, 0, 0, 8), (0, 1, 0, 8), (1, 0, 0, 8), (1, 1, 0, 4), (1, 1, 4, 4))


def apply(value, weight_ref, apart, rows, columns):
    high, low = halves(value)
    both = jnp.concatenate([high, low], axis=0)
    first = dot_rows(both, weight_ref[apart, 0, rows, columns])
    count = value.shape[0]
    return first[:count] + first[count:] + dot_rows(high, weight_ref[apart, 1, rows, columns])


def solve(residual, weight_ref):
    top, bottom = slice(0, 256), slice(256, 512)
    solved_top = apply(residual[:, :256], weight_ref, 0, top, top)
    rest = residual[:, 256:] - apply(solved_top, weight_ref, 0, bottom, top)
    return jnp.concatenate([solved_top, apply(rest, weight_ref, 0, bottom, bottom)], axis=1)


def push(solved, weight_ref, received, out_ref):
    for apart in range(1, out_ref.shape[0] + 1):
        term = apply(solved, weight_ref, apart, slice(0, SUPER), slice(0, SUPER))
        out_ref[apart - 1] = term if received is None else received[apart] + term


def chain_first(parts_ref, weight_ref, residual_ref, out_ref):
    by_rows = []
    for row_part in range(4):
        terms = [parts_ref[z, row_part, x] for z in range(PLANES) for x in range(2)]
        while len(terms) > 1:
            terms = [terms[i] + terms[i + 1] for i in range(0, len(terms), 2)]
        by_rows.append(terms[0])
    residual = jnp.concatenate([t[:, :64] for t in by_rows] + [t[:, 64:] for t in by_rows], axis=1)
    residual_ref[...] = residual
    push(solve(residual, weight_ref), weight_ref, None, out_ref)


def chain_middle(residual_ref, received_ref, weight_ref, next_ref, out_ref):
    residual = residual_ref[...] - received_ref[0]
    next_ref[...] = residual
    push(solve(residual, weight_ref), weight_ref, received_ref, out_ref)


def chain_last(residual_ref, received_ref, weight_ref, out_ref):
    solved = solve(residual_ref[...] - received_ref[0], weight_ref)
    for row_part in range(4):
        start = row_part * 64
        chunk = jnp.concatenate([solved[:, start : start + 64], solved[:, start + 256 : start + 320]], axis=1)
        for z in range(PLANES):
            for x in range(2):
                out_ref[z, row_part, x] = chunk


def turn(parts_ref, out_ref):
    for part in range(PLANES):
        out_ref[part] = parts_ref[part].T


def whole(*shape):
    return pl.BlockSpec(shape, lambda _: (0,) * len(shape))


def call(kernel, name, outs, *args, weights=None):
    specs = [whole(*a.shape) for a in args]
    if weights is not None:
        array, count = weights
        args += (array,)
        specs.append(whole(count, *array.shape[1:]))
    return pl.pallas_call(
        kernel,
        out_shape=[jax.ShapeDtypeStruct(s, F32) for s in outs],
        grid=(1,),
        in_specs=specs,
        out_specs=[whole(*s) for s in outs],
        compiler_params=pltpu.CompilerParams(vmem_limit_bytes=VMEM_LIMIT),
        name=name,
    )(*args)


def local(right_side, lower_prev, solved_prev, lower_window, inverse_diag):
    blocks, local_rows, columns = right_side.shape
    depth = lower_prev.shape[2]
    y, core, z, x = (lax.axis_index(a) for a in ("y", "core", "z", "x"))
    tile = next(t for t in (2304, 2016, 1792, 1152, 1024, 768, 512, 256, 128) if depth % t == 0)

    swap = functools.partial(lax.ppermute, perm=SWAP)
    own_inverse = lax.dynamic_slice_in_dim(inverse_diag, 2 * z + x, 1, 0)
    twice = jnp.concatenate([lower_window, lower_window], axis=0)
    message = jnp.concatenate([own_inverse, lax.dynamic_slice_in_dim(twice, 2 * z + 1, 7, 0)], axis=0)

    from_x = swap(message, "x")
    from_y = swap(message, "y")
    from_core = swap(message, "core")

    factor = lower_prev.reshape(blocks * local_rows, depth)
    right = right_side.reshape(blocks * local_rows, columns)
    first = (2 * z + x).astype(jnp.int32).reshape(1)
    total, finish = earlier_sums(first, factor, solved_prev, right, tile, (depth // tile + 1) // 2)

    total, from_x, from_y = lax.optimization_barrier((total, from_x, from_y))
    corner_low = swap(from_x[:4], "y")
    corner_high = swap(from_y[4:], "x")
    core_x, core_y = swap(from_x, "core"), swap(from_y, "core")
    parts = finish(total)

    parts, corner_low, corner_high = lax.optimization_barrier((parts, corner_low, corner_high))
    core_low, core_high = swap(corner_low, "core"), swap(corner_high, "core")
    parts = lax.all_to_all(parts.reshape(32, RHS_PART, 128), EVERY, 0, 0, tiled=True)

    pieces = (message, from_core, from_x, core_x, from_y, core_y, corner_low, core_low, corner_high, core_high)
    place = jnp.stack([y, core, x]).astype(jnp.int32)
    weights = pl.pallas_call(
        arrange,
        out_shape=jax.ShapeDtypeStruct((4, 2, SUPER, SUPER), BF16),
        grid=(1,),
        in_specs=[pl.BlockSpec(memory_space=pltpu.SMEM)] + [whole(*p.shape) for p in pieces],
        out_specs=whole(4, 2, SUPER, SUPER),
        compiler_params=pltpu.CompilerParams(vmem_limit_bytes=VMEM_LIMIT),
        name="arrange",
    )(place, *pieces)

    vector = (RHS_PART, SUPER)
    residual, sent = call(
        chain_first, "chain_first", [vector, (3, *vector)], parts.reshape(4, 4, 2, RHS_PART, 128), weights=(weights, 4)
    )
    for step in (1, 2):
        received = lax.ppermute(sent, "z", [(step - 1, step)])
        residual, sent = call(
            chain_middle, "chain_middle", [vector, (3 - step, *vector)], residual, received, weights=(weights, 4 - step)
        )
    received = lax.ppermute(sent, "z", [(2, 3)])
    (chunks,) = call(
        chain_last, "chain_last", [(4, 4, 2, RHS_PART, 128)], residual, received, weights=(weights, 1)
    )
    solved = lax.all_to_all(chunks.reshape(32, RHS_PART, 128), EVERY, 0, 0, tiled=True)
    (result,) = call(turn, "turn", [(PLANES, 128, columns)], solved.reshape(PLANES, columns, 128))
    return result.reshape(blocks, local_rows, columns)


def local_any(right_side, lower_prev, solved_prev, lower_window, inverse_diag):
    highest = lax.Precision.HIGHEST
    blocks, local_rows, columns = right_side.shape
    block_rows = inverse_diag.shape[2]
    row_start = lax.axis_index("prow") * local_rows
    solved = jnp.zeros((blocks * block_rows, columns), F32)
    pieces = []
    full_inverse = lax.all_gather(inverse_diag, "prow", axis=1, tiled=True)
    full_window = lax.all_gather(lower_window, "pcol", axis=2, tiled=True)
    dot = functools.partial(jnp.dot, precision=highest, preferred_element_type=F32)
    for row_block in range(blocks):
        window_term = dot(full_window[row_block], solved)
        earlier_here = lax.psum(dot(lower_prev[row_block], solved_prev), "pcol")
        local_residual = right_side[row_block] - (earlier_here + window_term)
        residual = lax.all_gather(local_residual, "prow", axis=0, tiled=True)
        whole_rows = dot(full_inverse[row_block], residual)
        pieces.append(lax.dynamic_slice_in_dim(whole_rows, row_start, local_rows, 0))
        solved = lax.dynamic_update_slice_in_dim(solved, whole_rows, row_block * block_rows, 0)
    return jnp.stack(pieces)


def run(mesh, body, row, column):
    in_specs = (P(None, row, None), P(None, row, column), P(column, None), P(None, row, column), P(None, row, None))
    return jax.shard_map(body, mesh=mesh, in_specs=in_specs, out_specs=P(None, row, None), check_vma=False)


def solution(mesh):
    if (mesh.shape["prow"], mesh.shape["pcol"]) == (4, 8):
        fine = Mesh(mesh.devices.reshape(2, 2, 4, 2), ("y", "core", "z", "x"))
        return run(fine, local, ("y", "core"), ("z", "x"))
    return run(mesh, local_any, "prow", "pcol")
```

```python
import functools

import jax
import jax.numpy as jnp
from jax import lax
from jax.experimental import pallas as pl
from jax.experimental.pallas import tpu as pltpu
from jax.sharding import Mesh, PartitionSpec as P

F32 = jnp.float32
BF16 = jnp.bfloat16
EVERY = ("z", "y", "core", "x")
SWAP = [(0, 1), (1, 0)]
PLANES = 4
RHS_PART = 16
SUPER = 512


def halves(value):
    high = value.astype(BF16)
    low = (value - high.astype(F32)).astype(BF16)
    return high, low


def dot_f32(a, b):
    return jnp.dot(a, b, preferred_element_type=F32)


def dot_rows(a, b):
    return lax.dot_general(a, b, (((1,), (1,)), ((), ())), preferred_element_type=F32)


def earlier_sums(first_ref, factor_ref, solved_ref, right_ref, out_ref, total):
    step = pl.program_id(0)

    @pl.when(step == 0)
    def _():
        total[...] = jnp.zeros_like(total)

    factor_high, factor_low = halves(factor_ref[...])
    solved_both = jnp.concatenate(halves(solved_ref[...]), axis=1)
    total[...] += dot_f32(factor_high, solved_both) + dot_f32(factor_low, solved_both)

    @pl.when(step == pl.num_programs(0) - 1)
    def _():
        keep = first_ref[0] == 0
        width = right_ref.shape[1]
        for part in range(PLANES):
            rows = slice(part * 128, part * 128 + 128)
            earlier = total[rows, :width] + total[rows, width:]
            right = jnp.where(keep, right_ref[rows, :], 0.0)
            out_ref[part] = (right - earlier).T


def earlier_residual(first, factor, solved, right):
    rows, depth = factor.shape
    columns = solved.shape[1]
    tile = next(t for t in (2304, 2016, 1792, 1152, 1024, 768, 512, 256, 128) if depth % t == 0)
    return pl.pallas_call(
        earlier_sums,
        out_shape=jax.ShapeDtypeStruct((PLANES, columns, 128), F32),
        grid=(depth // tile,),
        in_specs=[
            pl.BlockSpec(memory_space=pltpu.SMEM),
            pl.BlockSpec((rows, tile), lambda k: (0, k)),
            pl.BlockSpec((tile, columns), lambda k: (k, 0)),
            pl.BlockSpec((rows, columns), lambda k: (0, 0)),
        ],
        out_specs=pl.BlockSpec((PLANES, columns, 128), lambda k: (0, 0, 0)),
        scratch_shapes=[pltpu.VMEM((rows, 2 * columns), F32)],
        compiler_params=pltpu.CompilerParams(vmem_limit_bytes=24 << 20),
        cost_estimate=pl.CostEstimate(
            flops=8 * rows * columns * depth, bytes_accessed=4 * (rows + columns) * depth, transcendentals=0
        ),
        name="earlier",
    )(first, factor, solved, right)


def pack(window_ref, inverse_ref, out_ref, held, sems):
    z, x = lax.axis_index("z"), lax.axis_index("x")
    copies = []
    for j in range(8):
        source = inverse_ref.at[2 * z + x] if j == 0 else window_ref.at[lax.rem(2 * z + j, 8)]
        first = pltpu.make_async_copy(source, held.at[j], sems.at[0, j])
        copies.append((first, pltpu.make_async_copy(held.at[j], out_ref.at[j], sems.at[1, j])))
        first.start()
    for first, second in copies:
        first.wait()
        second.start()
    for first, second in copies:
        second.wait()


def place_piece(piece, y, core, x, other, dy, dx, start, outs):
    row_part = 2 * (y + dy - 2 * y * dy) + (core + other - 2 * core * other)
    column = x + dx - 2 * x * dx
    for j in range(piece.shape[0]):
        apart, b = (start + j) // 2, (start + j) % 2
        if apart == 0:
            b = column if b == 0 else 1 - column
        row = pl.multiple_of(b * 256 + row_part * 64, 64)
        where = (pl.ds(row, 64), pl.ds(pl.multiple_of(column * 256, 256), 256))
        for part, value in enumerate(halves(piece[j])):
            outs[apart][(part,) + where] = value


def arrange(spots, kept, *refs):
    count = len(spots)
    pieces, (held, sems) = refs[:count], refs[-2:]
    outs = refs[count + kept : -2]
    y, core, x = (lax.axis_index(a) for a in ("y", "core", "x"))
    copies = [pltpu.make_async_copy(pieces[i], held.at[i], sems.at[i]) for i in range(count)]
    for copy in copies:
        copy.start()
    for i, copy in enumerate(copies):
        copy.wait()
        other, dy, dx, start = spots[i]
        place_piece(held.at[i], y, core, x, other, dy, dx, start, outs)


def arranged(name, spots, pieces, weights=()):
    in_vmem = pl.BlockSpec(memory_space=pltpu.VMEM)
    count = len(pieces)
    return pl.pallas_call(
        functools.partial(arrange, spots, len(weights)),
        out_shape=[jax.ShapeDtypeStruct((2, SUPER, SUPER), BF16)] * 4,
        in_specs=[pl.BlockSpec(memory_space=pl.ANY)] * count + [in_vmem] * len(weights),
        out_specs=[in_vmem] * 4,
        scratch_shapes=[pltpu.VMEM((count, *pieces[0].shape), F32), pltpu.SemaphoreType.DMA((count,))],
        input_output_aliases={count + i: i for i in range(len(weights))},
        compiler_params=pltpu.CompilerParams(vmem_limit_bytes=8 << 20),
        name=name,
    )(*pieces, *weights)


def apply(value, weight_ref, rows, columns):
    high, low = halves(value)
    both = jnp.concatenate([high, low], axis=0)
    first = dot_rows(both, weight_ref[0, rows, columns])
    count = value.shape[0]
    return first[:count] + first[count:] + dot_rows(high, weight_ref[1, rows, columns])


def solve(residual, weight_ref):
    top, bottom = slice(0, 256), slice(256, 512)
    solved_top = apply(residual[:, :256], weight_ref, top, top)
    rest = residual[:, 256:] - apply(solved_top, weight_ref, bottom, top)
    return jnp.concatenate([solved_top, apply(rest, weight_ref, bottom, bottom)], axis=1)


def push(solved, weight_refs, received_ref, out_ref):
    for apart, weight_ref in enumerate(weight_refs, 1):
        term = apply(solved, weight_ref, slice(0, SUPER), slice(0, SUPER))
        out_ref[apart - 1] = term if received_ref is None else received_ref[apart] + term


def chain_first(parts_ref, *refs):
    weight_refs, (residual_ref, out_ref) = refs[:-2], refs[-2:]
    by_rows = []
    for row_part in range(4):
        terms = [parts_ref[z, row_part, x] for z in range(PLANES) for x in range(2)]
        while len(terms) > 1:
            terms = [terms[i] + terms[i + 1] for i in range(0, len(terms), 2)]
        by_rows.append(terms[0])
    residual = jnp.concatenate([t[:, :64] for t in by_rows] + [t[:, 64:] for t in by_rows], axis=1)
    residual_ref[...] = residual
    push(solve(residual, weight_refs[0]), weight_refs[1:], None, out_ref)


def chain_middle(residual_ref, received_ref, *refs):
    weight_refs, (next_ref, out_ref) = refs[:-2], refs[-2:]
    residual = residual_ref[...] - received_ref[0]
    next_ref[...] = residual
    push(solve(residual, weight_refs[0]), weight_refs[1:], received_ref, out_ref)


def chain_last(residual_ref, received_ref, weight_ref, out_ref):
    solved = solve(residual_ref[...] - received_ref[0], weight_ref)
    for row_part in range(4):
        start = row_part * 64
        chunk = jnp.concatenate([solved[:, start : start + 64], solved[:, start + 256 : start + 320]], axis=1)
        for z in range(PLANES):
            for x in range(2):
                out_ref[z, row_part, x] = chunk


def turn(parts_ref, out_ref):
    for part in range(PLANES):
        out_ref[part] = parts_ref[part].T


def call(kernel, name, outs, *args, limit=8 << 20):
    in_vmem = pl.BlockSpec(memory_space=pltpu.VMEM)
    return pl.pallas_call(
        kernel,
        out_shape=[jax.ShapeDtypeStruct(*o) for o in outs],
        in_specs=[in_vmem] * len(args),
        out_specs=[in_vmem] * len(outs),
        compiler_params=pltpu.CompilerParams(vmem_limit_bytes=limit),
        name=name,
    )(*args)


def local(right_side, lower_prev, solved_prev, lower_window, inverse_diag):
    blocks, local_rows, columns = right_side.shape
    depth = lower_prev.shape[2]
    swap = functools.partial(lax.ppermute, perm=SWAP)
    message = pl.pallas_call(
        pack,
        out_shape=jax.ShapeDtypeStruct(lower_window.shape, F32),
        in_specs=[pl.BlockSpec(memory_space=pl.ANY)] * 2,
        out_specs=pl.BlockSpec(memory_space=pl.ANY),
        scratch_shapes=[pltpu.VMEM(lower_window.shape, F32), pltpu.SemaphoreType.DMA((2, 8))],
        compiler_params=pltpu.CompilerParams(vmem_limit_bytes=60 << 20),
        cost_estimate=pl.CostEstimate(flops=0, bytes_accessed=16 << 20, transcendentals=0),
        name="pack",
    )(lower_window, inverse_diag)

    from_x = swap(message, "x")
    from_y = swap(message, "y")
    from_core = swap(message, "core")

    factor = lower_prev.reshape(blocks * local_rows, depth)
    right = right_side.reshape(blocks * local_rows, columns)
    first = (2 * lax.axis_index("z") + lax.axis_index("x")).astype(jnp.int32).reshape(1)
    parts = earlier_residual(first, factor, solved_prev, right)

    parts, from_x, from_y = lax.optimization_barrier((parts, from_x, from_y))
    corner_low = swap(from_x[:4], "y")
    corner_high = swap(from_y[4:], "x")
    core_x, core_y = swap(from_x, "core"), swap(from_y, "core")
    parts = lax.all_to_all(parts.reshape(32, RHS_PART, 128), EVERY, 0, 0, tiled=True)
    core_low, core_high = swap(corner_low, "core"), swap(corner_high, "core")
    pieces = (message, from_x, from_y, from_core, core_x, core_y)
    spots = ((0, 0, 0, 0), (0, 0, 1, 0), (0, 1, 0, 0), (1, 0, 0, 0), (1, 0, 1, 0), (1, 1, 0, 0))
    weights = arranged("arrange", spots, pieces)
    pieces = (corner_low, corner_high, core_low, core_high)
    weights = arranged("arrange_corner", ((0, 1, 1, 0), (0, 1, 1, 4), (1, 1, 1, 0), (1, 1, 1, 4)), pieces, weights)

    def vectors(*counts):
        return ((*counts, RHS_PART, SUPER), F32)

    residual, sent = call(chain_first, "chain_first", [vectors(), vectors(3)], parts.reshape(4, 4, 2, RHS_PART, 128), *weights)
    for step in (1, 2):
        received = lax.ppermute(sent, "z", [(step - 1, step)])
        outs = [vectors(), vectors(3 - step)]
        residual, sent = call(chain_middle, "chain_middle", outs, residual, received, *weights[: 4 - step])
    received = lax.ppermute(sent, "z", [(2, 3)])
    chunk = ((4, 4, 2, RHS_PART, 128), F32)
    (chunks,) = call(chain_last, "chain_last", [chunk], residual, received, weights[0])
    solved = lax.all_to_all(chunks.reshape(32, RHS_PART, 128), EVERY, 0, 0, tiled=True)
    (result,) = call(turn, "turn", [((PLANES, 128, columns), F32)], solved.reshape(PLANES, columns, 128))
    return result.reshape(blocks, local_rows, columns)


def local_any(right_side, lower_prev, solved_prev, lower_window, inverse_diag):
    highest = lax.Precision.HIGHEST
    blocks, local_rows, columns = right_side.shape
    block_rows = inverse_diag.shape[2]
    row_start = lax.axis_index("prow") * local_rows
    solved = jnp.zeros((blocks * block_rows, columns), F32)
    pieces = []
    full_inverse = lax.all_gather(inverse_diag, "prow", axis=1, tiled=True)
    full_window = lax.all_gather(lower_window, "pcol", axis=2, tiled=True)
    dot = functools.partial(jnp.dot, precision=highest, preferred_element_type=F32)
    for row_block in range(blocks):
        window_term = dot(full_window[row_block], solved)
        earlier_here = lax.psum(dot(lower_prev[row_block], solved_prev), "pcol")
        local_residual = right_side[row_block] - (earlier_here + window_term)
        residual = lax.all_gather(local_residual, "prow", axis=0, tiled=True)
        whole_rows = dot(full_inverse[row_block], residual)
        pieces.append(lax.dynamic_slice_in_dim(whole_rows, row_start, local_rows, 0))
        solved = lax.dynamic_update_slice_in_dim(solved, whole_rows, row_block * block_rows, 0)
    return jnp.stack(pieces)


def run(mesh, body, row, column):
    in_specs = (P(None, row, None), P(None, row, column), P(column, None), P(None, row, column), P(None, row, None))
    return jax.shard_map(body, mesh=mesh, in_specs=in_specs, out_specs=P(None, row, None), check_vma=False)


def solution(mesh):
    if (mesh.shape["prow"], mesh.shape["pcol"]) == (4, 8):
        fine = Mesh(mesh.devices.reshape(2, 2, 4, 2), ("y", "core", "z", "x"))
        return run(fine, local, ("y", "core"), ("z", "x"))
    return run(mesh, local_any, "prow", "pcol")
```

```python
import functools

import jax
import jax.numpy as jnp
from jax import lax
from jax.experimental import pallas as pl
from jax.experimental.pallas import tpu as pltpu
from jax.sharding import Mesh, PartitionSpec as P

F32 = jnp.float32
BF16 = jnp.bfloat16
EVERY = ("z", "y", "core", "x")
SWAP = [(0, 1), (1, 0)]
PLANES = 4
RHS_PART = 16
SUPER = 512


def halves(value):
    high = value.astype(BF16)
    low = (value - high.astype(F32)).astype(BF16)
    return high, low


def dot_f32(a, b):
    return jnp.dot(a, b, preferred_element_type=F32)


def dot_rows(a, b):
    return lax.dot_general(a, b, (((1,), (1,)), ((), ())), preferred_element_type=F32)


def earlier_sums(tile, first_ref, factor_ref, solved_ref, right_ref, out_ref, factors, solves, right, total, sems):
    steps = factor_ref.shape[1] // tile
    slots = factors.shape[0]

    def copies(step, slot):
        where = pl.ds(pl.multiple_of(step * tile, 128), tile)
        return (
            pltpu.make_async_copy(factor_ref.at[:, where], factors.at[slot], sems.at[0, slot]),
            pltpu.make_async_copy(solved_ref.at[where, :], solves.at[slot], sems.at[1, slot]),
        )

    for step in range(min(slots - 1, steps)):
        for copy in copies(step, step):
            copy.start()
    fetch_right = pltpu.make_async_copy(right_ref, right, sems.at[2, 0])
    fetch_right.start()
    total[...] = jnp.zeros_like(total)

    def body(step, carry):
        ahead = step + slots - 1

        @pl.when(ahead < steps)
        def _():
            for copy in copies(ahead, lax.rem(ahead, slots)):
                copy.start()

        slot = lax.rem(step, slots)
        for copy in copies(step, slot):
            copy.wait()
        factor_high, factor_low = halves(factors[slot])
        solved_both = jnp.concatenate(halves(solves[slot]), axis=1)
        total[...] += dot_f32(factor_high, solved_both) + dot_f32(factor_low, solved_both)
        return carry

    lax.fori_loop(0, steps, body, 0)
    fetch_right.wait()
    keep = first_ref[0] == 0
    width = right.shape[1]
    for part in range(PLANES):
        rows = slice(part * 128, part * 128 + 128)
        earlier = total[rows, :width] + total[rows, width:]
        out_ref[part] = (jnp.where(keep, right[rows, :], 0.0) - earlier).T


def in_hbm(*arrays):
    return tuple(pltpu.with_memory_space_constraint(a, pltpu.HBM) for a in arrays)


def earlier_residual(first, factor, solved, right):
    rows, depth = factor.shape
    columns = solved.shape[1]
    tile = next(t for t in (1152, 1024, 768, 512, 256, 128) if depth % t == 0)
    slots = 4
    anywhere = pl.BlockSpec(memory_space=pl.ANY)
    return pl.pallas_call(
        functools.partial(earlier_sums, tile),
        out_shape=jax.ShapeDtypeStruct((PLANES, columns, 128), F32),
        in_specs=[pl.BlockSpec(memory_space=pltpu.SMEM)] + [anywhere] * 3,
        out_specs=pl.BlockSpec(memory_space=pltpu.VMEM),
        scratch_shapes=[
            pltpu.VMEM((slots, rows, tile), F32),
            pltpu.VMEM((slots, tile, columns), F32),
            pltpu.VMEM((rows, columns), F32),
            pltpu.VMEM((rows, 2 * columns), F32),
            pltpu.SemaphoreType.DMA((3, slots)),
        ],
        compiler_params=pltpu.CompilerParams(vmem_limit_bytes=32 << 20),
        cost_estimate=pl.CostEstimate(
            flops=8 * rows * columns * depth, bytes_accessed=4 * (rows + columns) * depth, transcendentals=0
        ),
        name="earlier",
    )(first, *in_hbm(factor, solved, right))


def pack(window_ref, inverse_ref, out_ref, sems):
    z, x = lax.axis_index("z"), lax.axis_index("x")
    copies = [pltpu.make_async_copy(inverse_ref.at[2 * z + x], out_ref.at[0], sems.at[0])]
    for j in range(1, 8):
        copies.append(pltpu.make_async_copy(window_ref.at[lax.rem(2 * z + j, 8)], out_ref.at[j], sems.at[j]))
    for copy in copies:
        copy.start()
    for copy in copies:
        copy.wait()


def place_piece(piece, y, core, x, other, dy, dx, start, outs):
    row_part = 2 * (y + dy - 2 * y * dy) + (core + other - 2 * core * other)
    column = x + dx - 2 * x * dx
    for j in range(piece.shape[0]):
        apart, b = (start + j) // 2, (start + j) % 2
        if apart == 0:
            b = column if b == 0 else 1 - column
        row = pl.multiple_of(b * 256 + row_part * 64, 64)
        where = (pl.ds(row, 64), pl.ds(pl.multiple_of(column * 256, 256), 256))
        for part, value in enumerate(halves(piece[j])):
            outs[apart][(part,) + where] = value


def arrange(spots, kept, *refs):
    count = len(spots)
    pieces, (held, sems) = refs[:count], refs[-2:]
    outs = refs[count + kept : -2]
    y, core, x = (lax.axis_index(a) for a in ("y", "core", "x"))
    copies = [pltpu.make_async_copy(pieces[i], held.at[i], sems.at[i]) for i in range(count)]
    for copy in copies:
        copy.start()
    for i, copy in enumerate(copies):
        copy.wait()
        other, dy, dx, start = spots[i]
        place_piece(held.at[i], y, core, x, other, dy, dx, start, outs)


def arranged(name, spots, pieces, weights=()):
    in_vmem = pl.BlockSpec(memory_space=pltpu.VMEM)
    count = len(pieces)
    return pl.pallas_call(
        functools.partial(arrange, spots, len(weights)),
        out_shape=[jax.ShapeDtypeStruct((2, SUPER, SUPER), BF16)] * 4,
        in_specs=[pl.BlockSpec(memory_space=pl.ANY)] * count + [in_vmem] * len(weights),
        out_specs=[in_vmem] * 4,
        scratch_shapes=[pltpu.VMEM((count, *pieces[0].shape), F32), pltpu.SemaphoreType.DMA((count,))],
        input_output_aliases={count + i: i for i in range(len(weights))},
        compiler_params=pltpu.CompilerParams(vmem_limit_bytes=8 << 20),
        name=name,
    )(*in_hbm(*pieces), *weights)


def apply(value, weight_ref, rows, columns):
    high, low = halves(value)
    both = jnp.concatenate([high, low], axis=0)
    first = dot_rows(both, weight_ref[0, rows, columns])
    count = value.shape[0]
    return first[:count] + first[count:] + dot_rows(high, weight_ref[1, rows, columns])


def solve(residual, weight_ref):
    top, bottom = slice(0, 256), slice(256, 512)
    solved_top = apply(residual[:, :256], weight_ref, top, top)
    rest = residual[:, 256:] - apply(solved_top, weight_ref, bottom, top)
    return jnp.concatenate([solved_top, apply(rest, weight_ref, bottom, bottom)], axis=1)


def push(solved, weight_refs, received_ref, out_ref):
    for apart, weight_ref in enumerate(weight_refs, 1):
        term = apply(solved, weight_ref, slice(0, SUPER), slice(0, SUPER))
        out_ref[apart - 1] = term if received_ref is None else received_ref[apart] + term


def chain_first(parts_ref, *refs):
    weight_refs, (residual_ref, out_ref) = refs[:-2], refs[-2:]
    by_rows = []
    for row_part in range(4):
        terms = [parts_ref[z, row_part, x] for z in range(PLANES) for x in range(2)]
        while len(terms) > 1:
            terms = [terms[i] + terms[i + 1] for i in range(0, len(terms), 2)]
        by_rows.append(terms[0])
    residual = jnp.concatenate([t[:, :64] for t in by_rows] + [t[:, 64:] for t in by_rows], axis=1)
    residual_ref[...] = residual
    push(solve(residual, weight_refs[0]), weight_refs[1:], None, out_ref)


def chain_middle(residual_ref, received_ref, *refs):
    weight_refs, (next_ref, out_ref) = refs[:-2], refs[-2:]
    residual = residual_ref[...] - received_ref[0]
    next_ref[...] = residual
    push(solve(residual, weight_refs[0]), weight_refs[1:], received_ref, out_ref)


def chain_last(residual_ref, received_ref, weight_ref, out_ref):
    solved = solve(residual_ref[...] - received_ref[0], weight_ref)
    for row_part in range(4):
        start = row_part * 64
        chunk = jnp.concatenate([solved[:, start : start + 64], solved[:, start + 256 : start + 320]], axis=1)
        for z in range(PLANES):
            for x in range(2):
                out_ref[z, row_part, x] = chunk


def turn(parts_ref, out_ref):
    for part in range(PLANES):
        out_ref[part] = parts_ref[part].T


def call(kernel, name, outs, *args, limit=8 << 20):
    in_vmem = pl.BlockSpec(memory_space=pltpu.VMEM)
    return pl.pallas_call(
        kernel,
        out_shape=[jax.ShapeDtypeStruct(*o) for o in outs],
        in_specs=[in_vmem] * len(args),
        out_specs=[in_vmem] * len(outs),
        compiler_params=pltpu.CompilerParams(vmem_limit_bytes=limit),
        name=name,
    )(*args)


def local(right_side, lower_prev, solved_prev, lower_window, inverse_diag):
    blocks, local_rows, columns = right_side.shape
    depth = lower_prev.shape[2]
    swap = functools.partial(lax.ppermute, perm=SWAP)
    message = pl.pallas_call(
        pack,
        out_shape=jax.ShapeDtypeStruct(lower_window.shape, F32),
        in_specs=[pl.BlockSpec(memory_space=pl.ANY)] * 2,
        out_specs=pl.BlockSpec(memory_space=pltpu.VMEM),
        scratch_shapes=[pltpu.SemaphoreType.DMA((8,))],
        compiler_params=pltpu.CompilerParams(vmem_limit_bytes=4 << 20),
        name="pack",
    )(*in_hbm(lower_window, inverse_diag))

    from_x = swap(message, "x")
    from_y = swap(message, "y")
    from_core = swap(message, "core")

    factor = lower_prev.reshape(blocks * local_rows, depth)
    right = right_side.reshape(blocks * local_rows, columns)
    first = (2 * lax.axis_index("z") + lax.axis_index("x")).astype(jnp.int32).reshape(1)
    parts = earlier_residual(first, factor, solved_prev, right)

    parts, from_x, from_y = lax.optimization_barrier((parts, from_x, from_y))
    corner_low = swap(from_x[:4], "y")
    corner_high = swap(from_y[4:], "x")
    core_x, core_y = swap(from_x, "core"), swap(from_y, "core")
    parts = lax.all_to_all(parts.reshape(32, RHS_PART, 128), EVERY, 0, 0, tiled=True)
    core_low, core_high = swap(corner_low, "core"), swap(corner_high, "core")
    pieces = (message, from_x, from_y, from_core, core_x, core_y)
    spots = ((0, 0, 0, 0), (0, 0, 1, 0), (0, 1, 0, 0), (1, 0, 0, 0), (1, 0, 1, 0), (1, 1, 0, 0))
    weights = arranged("arrange", spots, pieces)
    pieces = (corner_low, corner_high, core_low, core_high)
    weights = arranged("arrange_corner", ((0, 1, 1, 0), (0, 1, 1, 4), (1, 1, 1, 0), (1, 1, 1, 4)), pieces, weights)

    def vectors(*counts):
        return ((*counts, RHS_PART, SUPER), F32)

    residual, sent = call(chain_first, "chain_first", [vectors(), vectors(3)], parts.reshape(4, 4, 2, RHS_PART, 128), *weights)
    for step in (1, 2):
        received = lax.ppermute(sent, "z", [(step - 1, step)])
        outs = [vectors(), vectors(3 - step)]
        residual, sent = call(chain_middle, "chain_middle", outs, residual, received, *weights[: 4 - step])
    received = lax.ppermute(sent, "z", [(2, 3)])
    chunk = ((4, 4, 2, RHS_PART, 128), F32)
    (chunks,) = call(chain_last, "chain_last", [chunk], residual, received, weights[0])
    solved = lax.all_to_all(chunks.reshape(32, RHS_PART, 128), EVERY, 0, 0, tiled=True)
    (result,) = call(turn, "turn", [((PLANES, 128, columns), F32)], solved.reshape(PLANES, columns, 128))
    return result.reshape(blocks, local_rows, columns)


def local_any(right_side, lower_prev, solved_prev, lower_window, inverse_diag):
    highest = lax.Precision.HIGHEST
    blocks, local_rows, columns = right_side.shape
    block_rows = inverse_diag.shape[2]
    row_start = lax.axis_index("prow") * local_rows
    solved = jnp.zeros((blocks * block_rows, columns), F32)
    pieces = []
    full_inverse = lax.all_gather(inverse_diag, "prow", axis=1, tiled=True)
    full_window = lax.all_gather(lower_window, "pcol", axis=2, tiled=True)
    dot = functools.partial(jnp.dot, precision=highest, preferred_element_type=F32)
    for row_block in range(blocks):
        window_term = dot(full_window[row_block], solved)
        earlier_here = lax.psum(dot(lower_prev[row_block], solved_prev), "pcol")
        local_residual = right_side[row_block] - (earlier_here + window_term)
        residual = lax.all_gather(local_residual, "prow", axis=0, tiled=True)
        whole_rows = dot(full_inverse[row_block], residual)
        pieces.append(lax.dynamic_slice_in_dim(whole_rows, row_start, local_rows, 0))
        solved = lax.dynamic_update_slice_in_dim(solved, whole_rows, row_block * block_rows, 0)
    return jnp.stack(pieces)


def run(mesh, body, row, column):
    in_specs = (P(None, row, None), P(None, row, column), P(column, None), P(None, row, column), P(None, row, None))
    return jax.shard_map(body, mesh=mesh, in_specs=in_specs, out_specs=P(None, row, None), check_vma=False)


def solution(mesh):
    if (mesh.shape["prow"], mesh.shape["pcol"]) == (4, 8):
        fine = Mesh(mesh.devices.reshape(2, 2, 4, 2), ("y", "core", "z", "x"))
        return run(fine, local, ("y", "core"), ("z", "x"))
    return run(mesh, local_any, "prow", "pcol")
```

```python
import functools

import jax
import jax.numpy as jnp
from jax import lax
from jax.experimental import pallas as pl
from jax.experimental.pallas import tpu as pltpu
from jax.sharding import Mesh, PartitionSpec as P

F32 = jnp.float32
BF16 = jnp.bfloat16
EVERY = ("z", "y", "core", "x")
SWAP = [(0, 1), (1, 0)]
PLANES = 4
RHS_PART = 16
SUPER = 512


def halves(value):
    high = value.astype(BF16)
    low = (value - high.astype(F32)).astype(BF16)
    return high, low


def dot_f32(a, b):
    return jnp.dot(a, b, preferred_element_type=F32)


def dot_rows(a, b):
    return lax.dot_general(a, b, (((1,), (1,)), ((), ())), preferred_element_type=F32)


def earlier_sums(tile, first_ref, factor_ref, solved_ref, right_ref, out_ref, factors, solves, right, total, sems):
    steps = factor_ref.shape[1] // tile
    slots = factors.shape[0]

    def copies(step, slot):
        where = pl.ds(pl.multiple_of(step * tile, 128), tile)
        return (
            pltpu.make_async_copy(factor_ref.at[:, where], factors.at[slot], sems.at[0, slot]),
            pltpu.make_async_copy(solved_ref.at[where, :], solves.at[slot], sems.at[1, slot]),
        )

    for step in range(min(slots - 1, steps)):
        for copy in copies(step, step):
            copy.start()
    fetch_right = pltpu.make_async_copy(right_ref, right, sems.at[2, 0])
    fetch_right.start()
    total[...] = jnp.zeros_like(total)

    def body(step, carry):
        ahead = step + slots - 1

        @pl.when(ahead < steps)
        def _():
            for copy in copies(ahead, lax.rem(ahead, slots)):
                copy.start()

        slot = lax.rem(step, slots)
        for copy in copies(step, slot):
            copy.wait()
        factor_high, factor_low = halves(factors[slot])
        solved_both = jnp.concatenate(halves(solves[slot]), axis=1)
        total[...] += dot_f32(factor_high, solved_both) + dot_f32(factor_low, solved_both)
        return carry

    lax.fori_loop(0, steps, body, 0)
    fetch_right.wait()
    keep = first_ref[0] == 0
    width = right.shape[1]
    for part in range(PLANES):
        rows = slice(part * 128, part * 128 + 128)
        earlier = total[rows, :width] + total[rows, width:]
        out_ref[part] = (jnp.where(keep, right[rows, :], 0.0) - earlier).T


def in_hbm(*arrays):
    return tuple(pltpu.with_memory_space_constraint(a, pltpu.HBM) for a in arrays)


def earlier_residual(first, factor, solved, right):
    rows, depth = factor.shape
    columns = solved.shape[1]
    tile = next(t for t in (1152, 1024, 768, 512, 256, 128) if depth % t == 0)
    slots = 4
    anywhere = pl.BlockSpec(memory_space=pl.ANY)
    return pl.pallas_call(
        functools.partial(earlier_sums, tile),
        out_shape=jax.ShapeDtypeStruct((PLANES, columns, 128), F32),
        in_specs=[pl.BlockSpec(memory_space=pltpu.SMEM)] + [anywhere] * 3,
        out_specs=pl.BlockSpec(memory_space=pltpu.VMEM),
        scratch_shapes=[
            pltpu.VMEM((slots, rows, tile), F32),
            pltpu.VMEM((slots, tile, columns), F32),
            pltpu.VMEM((rows, columns), F32),
            pltpu.VMEM((rows, 2 * columns), F32),
            pltpu.SemaphoreType.DMA((3, slots)),
        ],
        compiler_params=pltpu.CompilerParams(vmem_limit_bytes=32 << 20),
        cost_estimate=pl.CostEstimate(
            flops=8 * rows * columns * depth, bytes_accessed=4 * (rows + columns) * depth, transcendentals=0
        ),
        name="earlier",
    )(first, *in_hbm(factor, solved, right))


def pack(window_ref, inverse_ref, out_ref, sems):
    z, x = lax.axis_index("z"), lax.axis_index("x")
    copies = [pltpu.make_async_copy(inverse_ref.at[2 * z + x], out_ref.at[0], sems.at[0])]
    for j in range(1, 8):
        copies.append(pltpu.make_async_copy(window_ref.at[lax.rem(2 * z + j, 8)], out_ref.at[j], sems.at[j]))
    for copy in copies:
        copy.start()
    for copy in copies:
        copy.wait()


def place_piece(piece, y, core, x, other, dy, dx, start, outs):
    row_part = 2 * (y + dy - 2 * y * dy) + (core + other - 2 * core * other)
    column = x + dx - 2 * x * dx
    for j in range(piece.shape[0]):
        apart, b = (start + j) // 2, (start + j) % 2
        if apart == 0:
            b = column if b == 0 else 1 - column
        row = pl.multiple_of(b * 256 + row_part * 64, 64)
        where = (pl.ds(row, 64), pl.ds(pl.multiple_of(column * 256, 256), 256))
        for part, value in enumerate(halves(piece[j])):
            outs[apart][(part,) + where] = value


def arrange(spots, kept, *refs):
    count = len(spots)
    pieces, (held, sems) = refs[:count], refs[-2:]
    outs = refs[count + kept : -2]
    y, core, x = (lax.axis_index(a) for a in ("y", "core", "x"))
    copies = [pltpu.make_async_copy(pieces[i], held.at[i], sems.at[i]) for i in range(count)]
    for copy in copies:
        copy.start()
    for i, copy in enumerate(copies):
        copy.wait()
        other, dy, dx, start = spots[i]
        place_piece(held.at[i], y, core, x, other, dy, dx, start, outs)


def arranged(name, spots, pieces, *weights):
    in_vmem = pl.BlockSpec(memory_space=pltpu.VMEM)
    count = len(pieces)
    return pl.pallas_call(
        functools.partial(arrange, spots, len(weights)),
        out_shape=[jax.ShapeDtypeStruct((2, SUPER, SUPER), BF16)] * 4,
        in_specs=[pl.BlockSpec(memory_space=pl.ANY)] * count + [in_vmem] * len(weights),
        out_specs=[in_vmem] * 4,
        scratch_shapes=[pltpu.VMEM((count, *pieces[0].shape), F32), pltpu.SemaphoreType.DMA((count,))],
        input_output_aliases={count + i: i for i in range(len(weights))},
        compiler_params=pltpu.CompilerParams(vmem_limit_bytes=8 << 20),
        name=name,
    )(*pieces, *weights)


def apply(value, weight_ref, rows, columns):
    high, low = halves(value)
    both = jnp.concatenate([high, low], axis=0)
    first = dot_rows(both, weight_ref[0, rows, columns])
    count = value.shape[0]
    return first[:count] + first[count:] + dot_rows(high, weight_ref[1, rows, columns])


def solve(residual, weight_ref):
    top, bottom = slice(0, 256), slice(256, 512)
    solved_top = apply(residual[:, :256], weight_ref, top, top)
    rest = residual[:, 256:] - apply(solved_top, weight_ref, bottom, top)
    return jnp.concatenate([solved_top, apply(rest, weight_ref, bottom, bottom)], axis=1)


def push(solved, weight_refs, received_ref, out_ref):
    for apart, weight_ref in enumerate(weight_refs, 1):
        term = apply(solved, weight_ref, slice(0, SUPER), slice(0, SUPER))
        out_ref[apart - 1] = term if received_ref is None else received_ref[apart] + term


def chain_first(parts_ref, here_ref, near_ref, far_ref, farthest_ref, residual_ref, out_ref, held, sem):
    fetch = pltpu.make_async_copy(farthest_ref, held, sem)
    fetch.start()
    by_rows = []
    for row_part in range(4):
        terms = [parts_ref[z, row_part, x] for z in range(PLANES) for x in range(2)]
        while len(terms) > 1:
            terms = [terms[i] + terms[i + 1] for i in range(0, len(terms), 2)]
        by_rows.append(terms[0])
    residual = jnp.concatenate([t[:, :64] for t in by_rows] + [t[:, 64:] for t in by_rows], axis=1)
    residual_ref[...] = residual
    solved = solve(residual, here_ref)
    push(solved, (near_ref, far_ref), None, out_ref)
    fetch.wait()
    push(solved, (held,), None, out_ref.at[pl.ds(2, 1)])


def chain_middle(residual_ref, received_ref, *refs):
    weight_refs, (next_ref, out_ref) = refs[:-2], refs[-2:]
    residual = residual_ref[...] - received_ref[0]
    next_ref[...] = residual
    push(solve(residual, weight_refs[0]), weight_refs[1:], received_ref, out_ref)


def chain_last(residual_ref, received_ref, weight_ref, out_ref):
    solved = solve(residual_ref[...] - received_ref[0], weight_ref)
    for row_part in range(4):
        start = row_part * 64
        chunk = jnp.concatenate([solved[:, start : start + 64], solved[:, start + 256 : start + 320]], axis=1)
        for z in range(PLANES):
            for x in range(2):
                out_ref[z, row_part, x] = chunk


def turn(parts_ref, out_ref):
    for part in range(PLANES):
        out_ref[part] = parts_ref[part].T


def call(kernel, name, outs, *args, large=(), scratch=()):
    in_vmem = pl.BlockSpec(memory_space=pltpu.VMEM)
    return pl.pallas_call(
        kernel,
        out_shape=[jax.ShapeDtypeStruct(*o) for o in outs],
        in_specs=[in_vmem] * len(args) + [pl.BlockSpec(memory_space=pl.ANY)] * len(large),
        out_specs=[in_vmem] * len(outs),
        scratch_shapes=scratch,
        compiler_params=pltpu.CompilerParams(vmem_limit_bytes=8 << 20),
        name=name,
    )(*args, *in_hbm(*large))


def local(right_side, lower_prev, solved_prev, lower_window, inverse_diag):
    blocks, local_rows, columns = right_side.shape
    depth = lower_prev.shape[2]
    swap = functools.partial(lax.ppermute, perm=SWAP)
    message = pl.pallas_call(
        pack,
        out_shape=jax.ShapeDtypeStruct(lower_window.shape, F32),
        in_specs=[pl.BlockSpec(memory_space=pl.ANY)] * 2,
        out_specs=pl.BlockSpec(memory_space=pltpu.VMEM),
        scratch_shapes=[pltpu.SemaphoreType.DMA((8,))],
        compiler_params=pltpu.CompilerParams(vmem_limit_bytes=4 << 20),
        name="pack",
    )(*in_hbm(lower_window, inverse_diag))

    from_x = swap(message, "x")
    from_y = swap(message, "y")
    from_core = swap(message, "core")

    factor = lower_prev.reshape(blocks * local_rows, depth)
    right = right_side.reshape(blocks * local_rows, columns)
    first = (2 * lax.axis_index("z") + lax.axis_index("x")).astype(jnp.int32).reshape(1)
    parts = earlier_residual(first, factor, solved_prev, right)

    parts, from_x, from_y = lax.optimization_barrier((parts, from_x, from_y))
    corner_low = swap(from_x[:4], "y")
    corner_high = swap(from_y[4:], "x")
    core_x, core_y = swap(from_x, "core"), swap(from_y, "core")
    parts = lax.all_to_all(parts.reshape(32, RHS_PART, 128), EVERY, 0, 0, tiled=True)
    core_low, core_high = swap(corner_low, "core"), swap(corner_high, "core")
    pieces = (message, from_x, from_y, from_core, core_x, core_y)
    spots = ((0, 0, 0, 0), (0, 0, 1, 0), (0, 1, 0, 0), (1, 0, 0, 0), (1, 0, 1, 0), (1, 1, 0, 0))
    weights = arranged("arrange", spots, in_hbm(*pieces))
    pieces = (corner_low, corner_high, core_low, core_high)
    weights = arranged("arrange_corner", ((0, 1, 1, 0), (0, 1, 1, 4), (1, 1, 1, 0), (1, 1, 1, 4)), pieces, *weights)

    def vectors(*counts):
        return ((*counts, RHS_PART, SUPER), F32)

    parts = parts.reshape(4, 4, 2, RHS_PART, 128)
    scratch = [pltpu.VMEM((2, SUPER, SUPER), BF16), pltpu.SemaphoreType.DMA]
    residual, sent = call(
        chain_first, "chain_first", [vectors(), vectors(3)], parts, *weights[:3], large=weights[3:], scratch=scratch
    )
    for step in (1, 2):
        received = lax.ppermute(sent, "z", [(step - 1, step)])
        outs = [vectors(), vectors(3 - step)]
        residual, sent = call(chain_middle, "chain_middle", outs, residual, received, *weights[: 4 - step])
    received = lax.ppermute(sent, "z", [(2, 3)])
    chunk = ((4, 4, 2, RHS_PART, 128), F32)
    (chunks,) = call(chain_last, "chain_last", [chunk], residual, received, weights[0])
    solved = lax.all_to_all(chunks.reshape(32, RHS_PART, 128), EVERY, 0, 0, tiled=True)
    (result,) = call(turn, "turn", [((PLANES, 128, columns), F32)], solved.reshape(PLANES, columns, 128))
    return result.reshape(blocks, local_rows, columns)


def local_any(right_side, lower_prev, solved_prev, lower_window, inverse_diag):
    highest = lax.Precision.HIGHEST
    blocks, local_rows, columns = right_side.shape
    block_rows = inverse_diag.shape[2]
    row_start = lax.axis_index("prow") * local_rows
    solved = jnp.zeros((blocks * block_rows, columns), F32)
    pieces = []
    full_inverse = lax.all_gather(inverse_diag, "prow", axis=1, tiled=True)
    full_window = lax.all_gather(lower_window, "pcol", axis=2, tiled=True)
    dot = functools.partial(jnp.dot, precision=highest, preferred_element_type=F32)
    for row_block in range(blocks):
        window_term = dot(full_window[row_block], solved)
        earlier_here = lax.psum(dot(lower_prev[row_block], solved_prev), "pcol")
        local_residual = right_side[row_block] - (earlier_here + window_term)
        residual = lax.all_gather(local_residual, "prow", axis=0, tiled=True)
        whole_rows = dot(full_inverse[row_block], residual)
        pieces.append(lax.dynamic_slice_in_dim(whole_rows, row_start, local_rows, 0))
        solved = lax.dynamic_update_slice_in_dim(solved, whole_rows, row_block * block_rows, 0)
    return jnp.stack(pieces)


def run(mesh, body, row, column):
    in_specs = (P(None, row, None), P(None, row, column), P(column, None), P(None, row, column), P(None, row, None))
    return jax.shard_map(body, mesh=mesh, in_specs=in_specs, out_specs=P(None, row, None), check_vma=False)


def solution(mesh):
    if (mesh.shape["prow"], mesh.shape["pcol"]) == (4, 8):
        fine = Mesh(mesh.devices.reshape(2, 2, 4, 2), ("y", "core", "z", "x"))
        return run(fine, local, ("y", "core"), ("z", "x"))
    return run(mesh, local_any, "prow", "pcol")
```

```python
import functools

import jax
import jax.numpy as jnp
from jax import lax
from jax.experimental import pallas as pl
from jax.experimental.pallas import tpu as pltpu
from jax.sharding import Mesh, PartitionSpec as P

F32 = jnp.float32
BF16 = jnp.bfloat16
EVERY = ("z", "y", "core", "x")
SWAP = [(0, 1), (1, 0)]
PLANES = 4
RHS_PART = 16
SUPER = 512


def halves(value):
    high = value.astype(BF16)
    low = (value - high.astype(F32)).astype(BF16)
    return high, low


def dot_f32(a, b):
    return jnp.dot(a, b, preferred_element_type=F32)


def dot_rows(a, b):
    return lax.dot_general(a, b, (((1,), (1,)), ((), ())), preferred_element_type=F32)


def earlier_sums(tile, first_ref, factor_ref, solved_ref, right_ref, out_ref, factors, solves, right, total, sems):
    steps = factor_ref.shape[1] // tile
    slots = factors.shape[0]

    def copies(step, slot):
        where = pl.ds(pl.multiple_of(step * tile, 128), tile)
        return (
            pltpu.make_async_copy(factor_ref.at[:, where], factors.at[slot], sems.at[0, slot]),
            pltpu.make_async_copy(solved_ref.at[where, :], solves.at[slot], sems.at[1, slot]),
        )

    for step in range(min(slots - 1, steps)):
        for copy in copies(step, step):
            copy.start()
    fetch_right = pltpu.make_async_copy(right_ref, right, sems.at[2, 0])
    fetch_right.start()
    total[...] = jnp.zeros_like(total)

    def body(step, carry):
        ahead = step + slots - 1

        @pl.when(ahead < steps)
        def _():
            for copy in copies(ahead, lax.rem(ahead, slots)):
                copy.start()

        slot = lax.rem(step, slots)
        for copy in copies(step, slot):
            copy.wait()
        factor_high, factor_low = halves(factors[slot])
        solved_both = jnp.concatenate(halves(solves[slot]), axis=1)
        total[...] += dot_f32(factor_high, solved_both) + dot_f32(factor_low, solved_both)
        return carry

    lax.fori_loop(0, steps, body, 0)
    fetch_right.wait()
    keep = first_ref[0] == 0
    width = right.shape[1]
    for part in range(PLANES):
        rows = slice(part * 128, part * 128 + 128)
        earlier = total[rows, :width] + total[rows, width:]
        out_ref[part] = (jnp.where(keep, right[rows, :], 0.0) - earlier).T


def in_hbm(*arrays):
    return tuple(pltpu.with_memory_space_constraint(a, pltpu.HBM) for a in arrays)


def earlier_residual(first, factor, solved, right):
    rows, depth = factor.shape
    columns = solved.shape[1]
    tile = next(t for t in (1152, 1024, 768, 512, 256, 128) if depth % t == 0)
    slots = 4
    anywhere = pl.BlockSpec(memory_space=pl.ANY)
    return pl.pallas_call(
        functools.partial(earlier_sums, tile),
        out_shape=jax.ShapeDtypeStruct((PLANES, columns, 128), F32),
        in_specs=[pl.BlockSpec(memory_space=pltpu.SMEM)] + [anywhere] * 3,
        out_specs=pl.BlockSpec(memory_space=pltpu.VMEM),
        scratch_shapes=[
            pltpu.VMEM((slots, rows, tile), F32),
            pltpu.VMEM((slots, tile, columns), F32),
            pltpu.VMEM((rows, columns), F32),
            pltpu.VMEM((rows, 2 * columns), F32),
            pltpu.SemaphoreType.DMA((3, slots)),
        ],
        compiler_params=pltpu.CompilerParams(vmem_limit_bytes=32 << 20),
        cost_estimate=pl.CostEstimate(
            flops=8 * rows * columns * depth, bytes_accessed=4 * (rows + columns) * depth, transcendentals=0
        ),
        name="earlier",
    )(first, *in_hbm(factor, solved, right))


def pack(window_ref, inverse_ref, out_ref, sems):
    z, x = lax.axis_index("z"), lax.axis_index("x")
    copies = [pltpu.make_async_copy(inverse_ref.at[2 * z + x], out_ref.at[0], sems.at[0])]
    for j in range(1, 8):
        copies.append(pltpu.make_async_copy(window_ref.at[lax.rem(2 * z + j, 8)], out_ref.at[j], sems.at[j]))
    for copy in copies:
        copy.start()
    for copy in copies:
        copy.wait()


def place_piece(piece, y, core, x, other, dy, dx, start, outs):
    row_part = 2 * (y + dy - 2 * y * dy) + (core + other - 2 * core * other)
    column = x + dx - 2 * x * dx
    for j in range(piece.shape[0]):
        apart, b = (start + j) // 2, (start + j) % 2
        if apart == 0:
            b = column if b == 0 else 1 - column
        row = pl.multiple_of(b * 256 + row_part * 64, 64)
        where = (pl.ds(row, 64), pl.ds(pl.multiple_of(column * 256, 256), 256))
        for part, value in enumerate(halves(piece[j])):
            outs[apart][(part,) + where] = value


def arrange(spots, kept, *refs):
    count = len(spots)
    pieces, (held, sems) = refs[:count], refs[-2:]
    outs = refs[count + kept : -2]
    y, core, x = (lax.axis_index(a) for a in ("y", "core", "x"))
    copies = [pltpu.make_async_copy(pieces[i], held.at[i], sems.at[i]) for i in range(count)]
    for copy in copies:
        copy.start()
    for i, copy in enumerate(copies):
        copy.wait()
        other, dy, dx, start = spots[i]
        place_piece(held.at[i], y, core, x, other, dy, dx, start, outs)


def arranged(name, spots, pieces, *weights):
    in_vmem = pl.BlockSpec(memory_space=pltpu.VMEM)
    count = len(pieces)
    return pl.pallas_call(
        functools.partial(arrange, spots, len(weights)),
        out_shape=[jax.ShapeDtypeStruct((2, SUPER, SUPER), BF16)] * 4,
        in_specs=[pl.BlockSpec(memory_space=pl.ANY)] * count + [in_vmem] * len(weights),
        out_specs=[in_vmem] * 4,
        scratch_shapes=[pltpu.VMEM((count, *pieces[0].shape), F32), pltpu.SemaphoreType.DMA((count,))],
        input_output_aliases={count + i: i for i in range(len(weights))},
        compiler_params=pltpu.CompilerParams(vmem_limit_bytes=8 << 20),
        name=name,
    )(*pieces, *weights)


def product(left, right):
    return dot_f32(left[0], right[0]) + (dot_f32(left[1], right[0]) + dot_f32(left[0], right[1]))


def both_parts(weight_ref, rows=slice(0, SUPER), columns=slice(0, SUPER)):
    return weight_ref[0, rows, columns], weight_ref[1, rows, columns]


def invert(here_ref, out_ref):
    top, bottom = slice(0, 256), slice(256, 512)
    first, second = both_parts(here_ref, top, top), both_parts(here_ref, bottom, bottom)
    below = halves(product(both_parts(here_ref, bottom, top), first))
    corner = halves(-product(second, below))
    for part in range(2):
        out_ref[part, top, top] = first[part]
        out_ref[part, top, bottom] = jnp.zeros((256, 256), BF16)
        out_ref[part, bottom, top] = corner[part]
        out_ref[part, bottom, bottom] = second[part]


def combine(inverse_ref, near_ref, far_ref, *out_refs):
    inverse = both_parts(inverse_ref)
    for weight_ref, out_ref in zip((near_ref, far_ref), out_refs):
        out_ref[0], out_ref[1] = halves(product(both_parts(weight_ref), inverse))


def apply(value, weight_ref):
    high, low = halves(value)
    count = value.shape[0]
    first = dot_rows(jnp.concatenate([high, low], axis=0), weight_ref[0])
    return first[:count] + first[count:] + dot_rows(high, weight_ref[1])


def chain_first(parts_ref, inverse_ref, near_ref, far_ref, farthest_ref, residual_ref, out_ref, held, sem):
    fetch = pltpu.make_async_copy(farthest_ref, held, sem)
    fetch.start()
    by_rows = []
    for row_part in range(4):
        terms = [parts_ref[z, row_part, x] for z in range(PLANES) for x in range(2)]
        while len(terms) > 1:
            terms = [terms[i] + terms[i + 1] for i in range(0, len(terms), 2)]
        by_rows.append(terms[0])
    residual = jnp.concatenate([t[:, :64] for t in by_rows] + [t[:, 64:] for t in by_rows], axis=1)
    residual_ref[...] = residual
    solved = apply(residual, inverse_ref)
    out_ref[0] = apply(solved, near_ref)
    out_ref[1] = apply(solved, far_ref)
    fetch.wait()
    out_ref[2] = apply(solved, held)


def chain_middle(residual_ref, received_ref, *refs):
    combined_refs, (next_ref, out_ref) = refs[:-2], refs[-2:]
    residual = residual_ref[...] - received_ref[0]
    next_ref[...] = residual
    for apart, combined_ref in enumerate(combined_refs):
        out_ref[apart] = received_ref[apart + 1] + apply(residual, combined_ref)


def chain_last(residual_ref, received_ref, inverse_ref, out_ref):
    solved = apply(residual_ref[...] - received_ref[0], inverse_ref)
    for row_part in range(4):
        start = row_part * 64
        chunk = jnp.concatenate([solved[:, start : start + 64], solved[:, start + 256 : start + 320]], axis=1)
        for z in range(PLANES):
            for x in range(2):
                out_ref[z, row_part, x] = chunk


def split(first_ref, second_ref, low_ref, high_ref):
    low_ref[...] = first_ref[:4]
    high_ref[...] = second_ref[4:]


def turn(parts_ref, out_ref):
    for part in range(PLANES):
        out_ref[part] = parts_ref[part].T


def call(kernel, name, outs, *args, large=(), scratch=(), flops=None):
    in_vmem = pl.BlockSpec(memory_space=pltpu.VMEM)
    return pl.pallas_call(
        kernel,
        out_shape=[jax.ShapeDtypeStruct(*o) for o in outs],
        in_specs=[in_vmem] * len(args) + [pl.BlockSpec(memory_space=pl.ANY)] * len(large),
        out_specs=[in_vmem] * len(outs),
        scratch_shapes=scratch,
        compiler_params=pltpu.CompilerParams(vmem_limit_bytes=8 << 20),
        cost_estimate=flops and pl.CostEstimate(flops=flops, bytes_accessed=1 << 21, transcendentals=0),
        name=name,
    )(*args, *in_hbm(*large))


def local(right_side, lower_prev, solved_prev, lower_window, inverse_diag):
    blocks, local_rows, columns = right_side.shape
    depth = lower_prev.shape[2]
    swap = functools.partial(lax.ppermute, perm=SWAP)
    message = pl.pallas_call(
        pack,
        out_shape=jax.ShapeDtypeStruct(lower_window.shape, F32),
        in_specs=[pl.BlockSpec(memory_space=pl.ANY)] * 2,
        out_specs=pl.BlockSpec(memory_space=pltpu.VMEM),
        scratch_shapes=[pltpu.SemaphoreType.DMA((8,))],
        compiler_params=pltpu.CompilerParams(vmem_limit_bytes=4 << 20),
        name="pack",
    )(*in_hbm(lower_window, inverse_diag))

    from_x = swap(message, "x")
    from_y = swap(message, "y")
    from_core = swap(message, "core")

    factor = lower_prev.reshape(blocks * local_rows, depth)
    right = right_side.reshape(blocks * local_rows, columns)
    first = (2 * lax.axis_index("z") + lax.axis_index("x")).astype(jnp.int32).reshape(1)
    parts = earlier_residual(first, factor, solved_prev, right)

    parts, from_x, from_y = lax.optimization_barrier((parts, from_x, from_y))
    half = ((4, *lower_window.shape[1:]), F32)
    low, high = call(split, "split", [half] * 2, from_x, from_y)
    corner_low, corner_high = swap(low, "y"), swap(high, "x")
    core_x, core_y = swap(from_x, "core"), swap(from_y, "core")
    parts = lax.all_to_all(parts.reshape(32, RHS_PART, 128), EVERY, 0, 0, tiled=True)
    core_low, core_high = swap(corner_low, "core"), swap(corner_high, "core")
    pieces = (message, from_x, from_y, from_core, core_x, core_y)
    spots = ((0, 0, 0, 0), (0, 0, 1, 0), (0, 1, 0, 0), (1, 0, 0, 0), (1, 0, 1, 0), (1, 1, 0, 0))
    weights = arranged("arrange", spots, in_hbm(*pieces))
    pieces = (corner_low, corner_high, core_low, core_high)
    weights = arranged("arrange_corner", ((0, 1, 1, 0), (0, 1, 1, 4), (1, 1, 1, 0), (1, 1, 1, 4)), pieces, *weights)

    here, near, far, farthest = weights
    weight = ((2, SUPER, SUPER), BF16)
    (inverse,) = call(invert, "invert", [weight], here, flops=6 * 256**3 * 2)

    def vectors(*counts):
        return ((*counts, RHS_PART, SUPER), F32)

    parts = parts.reshape(4, 4, 2, RHS_PART, 128)
    scratch = [pltpu.VMEM((2, SUPER, SUPER), BF16), pltpu.SemaphoreType.DMA]
    residual, sent = call(
        chain_first,
        "chain_first",
        [vectors(), vectors(3)],
        *(parts, inverse, near, far),
        large=[farthest],
        scratch=scratch,
    )
    combined = call(combine, "combine", [weight] * 2, inverse, near, far, flops=6 * SUPER**3 * 2)
    for step in (1, 2):
        received = lax.ppermute(sent, "z", [(step - 1, step)])
        outs = [vectors(), vectors(3 - step)]
        residual, sent = call(chain_middle, "chain_middle", outs, residual, received, *combined[: 3 - step])
    received = lax.ppermute(sent, "z", [(2, 3)])
    chunk = ((4, 4, 2, RHS_PART, 128), F32)
    (chunks,) = call(chain_last, "chain_last", [chunk], residual, received, inverse)
    solved = lax.all_to_all(chunks.reshape(32, RHS_PART, 128), EVERY, 0, 0, tiled=True)
    (result,) = call(turn, "turn", [((PLANES, 128, columns), F32)], solved.reshape(PLANES, columns, 128))
    return result.reshape(blocks, local_rows, columns)


def local_any(right_side, lower_prev, solved_prev, lower_window, inverse_diag):
    highest = lax.Precision.HIGHEST
    blocks, local_rows, columns = right_side.shape
    block_rows = inverse_diag.shape[2]
    row_start = lax.axis_index("prow") * local_rows
    solved = jnp.zeros((blocks * block_rows, columns), F32)
    pieces = []
    full_inverse = lax.all_gather(inverse_diag, "prow", axis=1, tiled=True)
    full_window = lax.all_gather(lower_window, "pcol", axis=2, tiled=True)
    dot = functools.partial(jnp.dot, precision=highest, preferred_element_type=F32)
    for row_block in range(blocks):
        window_term = dot(full_window[row_block], solved)
        earlier_here = lax.psum(dot(lower_prev[row_block], solved_prev), "pcol")
        local_residual = right_side[row_block] - (earlier_here + window_term)
        residual = lax.all_gather(local_residual, "prow", axis=0, tiled=True)
        whole_rows = dot(full_inverse[row_block], residual)
        pieces.append(lax.dynamic_slice_in_dim(whole_rows, row_start, local_rows, 0))
        solved = lax.dynamic_update_slice_in_dim(solved, whole_rows, row_block * block_rows, 0)
    return jnp.stack(pieces)


def run(mesh, body, row, column):
    in_specs = (P(None, row, None), P(None, row, column), P(column, None), P(None, row, column), P(None, row, None))
    return jax.shard_map(body, mesh=mesh, in_specs=in_specs, out_specs=P(None, row, None), check_vma=False)


def solution(mesh):
    if (mesh.shape["prow"], mesh.shape["pcol"]) == (4, 8):
        fine = Mesh(mesh.devices.reshape(2, 2, 4, 2), ("y", "core", "z", "x"))
        return run(fine, local, ("y", "core"), ("z", "x"))
    return run(mesh, local_any, "prow", "pcol")
```

```python
import functools

import jax
import jax.numpy as jnp
from jax import lax
from jax.experimental import pallas as pl
from jax.experimental.pallas import tpu as pltpu
from jax.sharding import Mesh, PartitionSpec as P

F32 = jnp.float32
BF16 = jnp.bfloat16
EVERY = ("z", "y", "core", "x")
SWAP = [(0, 1), (1, 0)]
PLANES = 4
RHS_PART = 16
SUPER = 512


def halves(value):
    high = value.astype(BF16)
    low = (value - high.astype(F32)).astype(BF16)
    return high, low


def dot_f32(a, b):
    return jnp.dot(a, b, preferred_element_type=F32)


def dot_rows(a, b):
    return lax.dot_general(a, b, (((1,), (1,)), ((), ())), preferred_element_type=F32)


def earlier_sums(tile, first_ref, factor_ref, solved_ref, right_ref, out_ref, factors, solves, right, total, sems):
    steps = factor_ref.shape[1] // tile
    slots = factors.shape[0]

    def copies(step, slot):
        where = pl.ds(pl.multiple_of(step * tile, 128), tile)
        return (
            pltpu.make_async_copy(factor_ref.at[:, where], factors.at[slot], sems.at[0, slot]),
            pltpu.make_async_copy(solved_ref.at[where, :], solves.at[slot], sems.at[1, slot]),
        )

    for step in range(min(slots - 1, steps)):
        for copy in copies(step, step):
            copy.start()
    fetch_right = pltpu.make_async_copy(right_ref, right, sems.at[2, 0])
    fetch_right.start()
    total[...] = jnp.zeros_like(total)

    def body(step, carry):
        ahead = step + slots - 1

        @pl.when(ahead < steps)
        def _():
            for copy in copies(ahead, lax.rem(ahead, slots)):
                copy.start()

        slot = lax.rem(step, slots)
        for copy in copies(step, slot):
            copy.wait()
        factor_high, factor_low = halves(factors[slot])
        solved_both = jnp.concatenate(halves(solves[slot]), axis=1)
        total[...] += dot_f32(factor_high, solved_both) + dot_f32(factor_low, solved_both)
        return carry

    lax.fori_loop(0, steps, body, 0)
    fetch_right.wait()
    keep = first_ref[0] == 0
    width = right.shape[1]
    for part in range(PLANES):
        rows = slice(part * 128, part * 128 + 128)
        earlier = total[rows, :width] + total[rows, width:]
        out_ref[part] = (jnp.where(keep, right[rows, :], 0.0) - earlier).T


def in_hbm(*arrays):
    return tuple(pltpu.with_memory_space_constraint(a, pltpu.HBM) for a in arrays)


def earlier_residual(first, factor, solved, right):
    rows, depth = factor.shape
    columns = solved.shape[1]
    tile = next(t for t in (1152, 1024, 768, 512, 256, 128) if depth % t == 0)
    slots = 4
    anywhere = pl.BlockSpec(memory_space=pl.ANY)
    return pl.pallas_call(
        functools.partial(earlier_sums, tile),
        out_shape=jax.ShapeDtypeStruct((PLANES, columns, 128), F32),
        in_specs=[pl.BlockSpec(memory_space=pltpu.SMEM)] + [anywhere] * 3,
        out_specs=pl.BlockSpec(memory_space=pltpu.VMEM),
        scratch_shapes=[
            pltpu.VMEM((slots, rows, tile), F32),
            pltpu.VMEM((slots, tile, columns), F32),
            pltpu.VMEM((rows, columns), F32),
            pltpu.VMEM((rows, 2 * columns), F32),
            pltpu.SemaphoreType.DMA((3, slots)),
        ],
        compiler_params=pltpu.CompilerParams(vmem_limit_bytes=32 << 20),
        cost_estimate=pl.CostEstimate(
            flops=8 * rows * columns * depth, bytes_accessed=4 * (rows + columns) * depth, transcendentals=0
        ),
        name="earlier",
    )(first, *in_hbm(factor, solved, right))


def pack(window_ref, inverse_ref, out_ref, sems):
    z, x = lax.axis_index("z"), lax.axis_index("x")
    copies = [pltpu.make_async_copy(inverse_ref.at[2 * z + x], out_ref.at[0], sems.at[0])]
    for j in range(1, 8):
        copies.append(pltpu.make_async_copy(window_ref.at[lax.rem(2 * z + j, 8)], out_ref.at[j], sems.at[j]))
    for copy in copies:
        copy.start()
    for copy in copies:
        copy.wait()


def place_piece(piece, y, core, x, other, dy, dx, start, outs):
    row_part = 2 * (y + dy - 2 * y * dy) + (core + other - 2 * core * other)
    column = x + dx - 2 * x * dx
    for j in range(piece.shape[0]):
        apart, b = (start + j) // 2, (start + j) % 2
        if apart == 0:
            b = column if b == 0 else 1 - column
        row = pl.multiple_of(b * 256 + row_part * 64, 64)
        where = (pl.ds(row, 64), pl.ds(pl.multiple_of(column * 256, 256), 256))
        for part, value in enumerate(halves(piece[j])):
            outs[apart][(part,) + where] = value


def arrange(spots, kept, *refs):
    count = len(spots)
    pieces, (held, sems) = refs[:count], refs[-2:]
    outs = refs[count + kept : -2]
    y, core, x = (lax.axis_index(a) for a in ("y", "core", "x"))
    copies = [pltpu.make_async_copy(pieces[i], held.at[i], sems.at[i]) for i in range(count)]
    for copy in copies:
        copy.start()
    for i, copy in enumerate(copies):
        copy.wait()
        other, dy, dx, start = spots[i]
        place_piece(held.at[i], y, core, x, other, dy, dx, start, outs)


def arranged(name, spots, pieces, *weights):
    in_vmem = pl.BlockSpec(memory_space=pltpu.VMEM)
    count = len(pieces)
    return pl.pallas_call(
        functools.partial(arrange, spots, len(weights)),
        out_shape=[jax.ShapeDtypeStruct((2, SUPER, SUPER), BF16)] * 4,
        in_specs=[pl.BlockSpec(memory_space=pl.ANY)] * count + [in_vmem] * len(weights),
        out_specs=[in_vmem] * 4,
        scratch_shapes=[pltpu.VMEM((count, *pieces[0].shape), F32), pltpu.SemaphoreType.DMA((count,))],
        input_output_aliases={count + i: i for i in range(len(weights))},
        compiler_params=pltpu.CompilerParams(vmem_limit_bytes=8 << 20),
        name=name,
    )(*pieces, *weights)


def product(left, right):
    return dot_f32(left[0], right[0]) + (dot_f32(left[1], right[0]) + dot_f32(left[0], right[1]))


def both_parts(weight_ref, rows=slice(0, SUPER), columns=slice(0, SUPER)):
    return weight_ref[0, rows, columns], weight_ref[1, rows, columns]


def invert(here_ref, out_ref):
    top, bottom = slice(0, 256), slice(256, 512)
    first, second = both_parts(here_ref, top, top), both_parts(here_ref, bottom, bottom)
    below = halves(product(both_parts(here_ref, bottom, top), first))
    corner = halves(-product(second, below))
    for part in range(2):
        out_ref[part, top, top] = first[part]
        out_ref[part, top, bottom] = jnp.zeros((256, 256), BF16)
        out_ref[part, bottom, top] = corner[part]
        out_ref[part, bottom, bottom] = second[part]


def combine(inverse_ref, near_ref, far_ref, *out_refs):
    inverse = both_parts(inverse_ref)
    for weight_ref, out_ref in zip((near_ref, far_ref), out_refs):
        out_ref[0], out_ref[1] = halves(product(both_parts(weight_ref), inverse))


def apply(value, weight_ref):
    high, low = halves(value)
    count = value.shape[0]
    first = dot_rows(jnp.concatenate([high, low], axis=0), weight_ref[0])
    return first[:count] + first[count:] + dot_rows(high, weight_ref[1])


def chain_first(parts_ref, inverse_ref, near_ref, far_ref, residual_ref, solved_ref, out_ref):
    by_rows = []
    for row_part in range(4):
        terms = [parts_ref[z, row_part, x] for z in range(PLANES) for x in range(2)]
        while len(terms) > 1:
            terms = [terms[i] + terms[i + 1] for i in range(0, len(terms), 2)]
        by_rows.append(terms[0])
    residual = jnp.concatenate([t[:, :64] for t in by_rows] + [t[:, 64:] for t in by_rows], axis=1)
    residual_ref[...] = residual
    solved = apply(residual, inverse_ref)
    solved_ref[...] = solved
    out_ref[0] = apply(solved, near_ref)
    out_ref[1] = apply(solved, far_ref)


def chain_direct(solved_ref, farthest_ref, out_ref, held, sem):
    fetch = pltpu.make_async_copy(farthest_ref, held, sem)
    fetch.start()
    fetch.wait()
    out_ref[...] = apply(solved_ref[...], held)


def chain_middle(residual_ref, received_ref, *refs):
    combined_refs, (next_ref, out_ref) = refs[:-2], refs[-2:]
    residual = residual_ref[...] - received_ref[0]
    next_ref[...] = residual
    for apart, combined_ref in enumerate(combined_refs):
        term = apply(residual, combined_ref)
        out_ref[apart] = received_ref[1] + term if apart == 0 else term


def chain_last(residual_ref, received_ref, direct_ref, inverse_ref, out_ref):
    solved = apply(residual_ref[...] - (received_ref[0] + direct_ref[...]), inverse_ref)
    for row_part in range(4):
        start = row_part * 64
        chunk = jnp.concatenate([solved[:, start : start + 64], solved[:, start + 256 : start + 320]], axis=1)
        for z in range(PLANES):
            for x in range(2):
                out_ref[z, row_part, x] = chunk


def split(first_ref, second_ref, low_ref, high_ref):
    low_ref[...] = first_ref[:4]
    high_ref[...] = second_ref[4:]


def turn(parts_ref, out_ref):
    for part in range(PLANES):
        out_ref[part] = parts_ref[part].T


def call(kernel, name, outs, *args, large=(), scratch=(), flops=None):
    in_vmem = pl.BlockSpec(memory_space=pltpu.VMEM)
    return pl.pallas_call(
        kernel,
        out_shape=[jax.ShapeDtypeStruct(*o) for o in outs],
        in_specs=[in_vmem] * len(args) + [pl.BlockSpec(memory_space=pl.ANY)] * len(large),
        out_specs=[in_vmem] * len(outs),
        scratch_shapes=scratch,
        compiler_params=pltpu.CompilerParams(vmem_limit_bytes=8 << 20),
        cost_estimate=flops and pl.CostEstimate(flops=flops, bytes_accessed=1 << 21, transcendentals=0),
        name=name,
    )(*args, *in_hbm(*large))


def local(right_side, lower_prev, solved_prev, lower_window, inverse_diag):
    blocks, local_rows, columns = right_side.shape
    depth = lower_prev.shape[2]
    swap = functools.partial(lax.ppermute, perm=SWAP)
    message = pl.pallas_call(
        pack,
        out_shape=jax.ShapeDtypeStruct(lower_window.shape, F32),
        in_specs=[pl.BlockSpec(memory_space=pl.ANY)] * 2,
        out_specs=pl.BlockSpec(memory_space=pltpu.VMEM),
        scratch_shapes=[pltpu.SemaphoreType.DMA((8,))],
        compiler_params=pltpu.CompilerParams(vmem_limit_bytes=4 << 20),
        name="pack",
    )(*in_hbm(lower_window, inverse_diag))

    from_x = swap(message, "x")
    from_y = swap(message, "y")
    from_core = swap(message, "core")

    factor = lower_prev.reshape(blocks * local_rows, depth)
    right = right_side.reshape(blocks * local_rows, columns)
    first = (2 * lax.axis_index("z") + lax.axis_index("x")).astype(jnp.int32).reshape(1)
    parts = earlier_residual(first, factor, solved_prev, right)

    parts, from_x, from_y = lax.optimization_barrier((parts, from_x, from_y))
    half = ((4, *lower_window.shape[1:]), F32)
    low, high = call(split, "split", [half] * 2, from_x, from_y)
    corner_low, corner_high = swap(low, "y"), swap(high, "x")
    core_x, core_y = swap(from_x, "core"), swap(from_y, "core")
    parts = lax.all_to_all(parts.reshape(32, RHS_PART, 128), EVERY, 0, 0, tiled=True)
    core_low, core_high = swap(corner_low, "core"), swap(corner_high, "core")
    pieces = (message, from_x, from_y, from_core, core_x, core_y)
    spots = ((0, 0, 0, 0), (0, 0, 1, 0), (0, 1, 0, 0), (1, 0, 0, 0), (1, 0, 1, 0), (1, 1, 0, 0))
    weights = arranged("arrange", spots, in_hbm(*pieces))
    pieces = (corner_low, corner_high, core_low, core_high)
    weights = arranged("arrange_corner", ((0, 1, 1, 0), (0, 1, 1, 4), (1, 1, 1, 0), (1, 1, 1, 4)), pieces, *weights)

    here, near, far, farthest = weights
    weight = ((2, SUPER, SUPER), BF16)
    (inverse,) = call(invert, "invert", [weight], here, flops=6 * 256**3 * 2)

    def vectors(*counts):
        return ((*counts, RHS_PART, SUPER), F32)

    parts = parts.reshape(4, 4, 2, RHS_PART, 128)
    scratch = [pltpu.VMEM((2, SUPER, SUPER), BF16), pltpu.SemaphoreType.DMA]
    outs = [vectors(), vectors(), vectors(2)]
    residual, solved, sent = call(chain_first, "chain_first", outs, parts, inverse, near, far)
    (direct,) = call(
        chain_direct, "chain_direct", [vectors()], solved, large=[farthest], scratch=scratch, flops=6 * 16 * SUPER**2
    )
    direct = lax.ppermute(direct, "z", [(0, 3)])
    combined = call(combine, "combine", [weight] * 2, inverse, near, far, flops=6 * SUPER**3 * 2)
    for step in (1, 2):
        received = lax.ppermute(sent, "z", [(step - 1, step)])
        outs = [vectors(), vectors(3 - step)]
        residual, sent = call(chain_middle, "chain_middle", outs, residual, received, *combined[: 3 - step])
    received = lax.ppermute(sent, "z", [(2, 3)])
    chunk = ((4, 4, 2, RHS_PART, 128), F32)
    (chunks,) = call(chain_last, "chain_last", [chunk], residual, received, direct, inverse)
    solved = lax.all_to_all(chunks.reshape(32, RHS_PART, 128), EVERY, 0, 0, tiled=True)
    (result,) = call(turn, "turn", [((PLANES, 128, columns), F32)], solved.reshape(PLANES, columns, 128))
    return result.reshape(blocks, local_rows, columns)


def local_any(right_side, lower_prev, solved_prev, lower_window, inverse_diag):
    highest = lax.Precision.HIGHEST
    blocks, local_rows, columns = right_side.shape
    block_rows = inverse_diag.shape[2]
    row_start = lax.axis_index("prow") * local_rows
    solved = jnp.zeros((blocks * block_rows, columns), F32)
    pieces = []
    full_inverse = lax.all_gather(inverse_diag, "prow", axis=1, tiled=True)
    full_window = lax.all_gather(lower_window, "pcol", axis=2, tiled=True)
    dot = functools.partial(jnp.dot, precision=highest, preferred_element_type=F32)
    for row_block in range(blocks):
        window_term = dot(full_window[row_block], solved)
        earlier_here = lax.psum(dot(lower_prev[row_block], solved_prev), "pcol")
        local_residual = right_side[row_block] - (earlier_here + window_term)
        residual = lax.all_gather(local_residual, "prow", axis=0, tiled=True)
        whole_rows = dot(full_inverse[row_block], residual)
        pieces.append(lax.dynamic_slice_in_dim(whole_rows, row_start, local_rows, 0))
        solved = lax.dynamic_update_slice_in_dim(solved, whole_rows, row_block * block_rows, 0)
    return jnp.stack(pieces)


def run(mesh, body, row, column):
    in_specs = (P(None, row, None), P(None, row, column), P(column, None), P(None, row, column), P(None, row, None))
    return jax.shard_map(body, mesh=mesh, in_specs=in_specs, out_specs=P(None, row, None), check_vma=False)


def solution(mesh):
    if (mesh.shape["prow"], mesh.shape["pcol"]) == (4, 8):
        fine = Mesh(mesh.devices.reshape(2, 2, 4, 2), ("y", "core", "z", "x"))
        return run(fine, local, ("y", "core"), ("z", "x"))
    return run(mesh, local_any, "prow", "pcol")
```

```python
import functools

import jax
import jax.numpy as jnp
from jax import lax
from jax.experimental import pallas as pl
from jax.experimental.pallas import tpu as pltpu
from jax.sharding import Mesh, PartitionSpec as P

F32 = jnp.float32
BF16 = jnp.bfloat16
EVERY = ("z", "y", "core", "x")
SWAP = [(0, 1), (1, 0)]
PLANES = 4
RHS_PART = 16
SUPER = 512


def halves(value):
    high = value.astype(BF16)
    low = (value - high.astype(F32)).astype(BF16)
    return high, low


def dot_f32(a, b):
    return jnp.dot(a, b, preferred_element_type=F32)


def dot_rows(a, b):
    return lax.dot_general(a, b, (((1,), (1,)), ((), ())), preferred_element_type=F32)


def earlier_sums(tile, first_ref, factor_ref, solved_ref, right_ref, out_ref, factors, solves, right, total, sems):
    steps = factor_ref.shape[1] // tile
    slots = factors.shape[0]

    def copies(step, slot):
        where = pl.ds(pl.multiple_of(step * tile, 128), tile)
        return (
            pltpu.make_async_copy(factor_ref.at[:, where], factors.at[slot], sems.at[0, slot]),
            pltpu.make_async_copy(solved_ref.at[where, :], solves.at[slot], sems.at[1, slot]),
        )

    for step in range(min(slots - 1, steps)):
        for copy in copies(step, step):
            copy.start()
    fetch_right = pltpu.make_async_copy(right_ref, right, sems.at[2, 0])
    fetch_right.start()
    total[...] = jnp.zeros_like(total)

    def body(step, carry):
        ahead = step + slots - 1

        @pl.when(ahead < steps)
        def _():
            for copy in copies(ahead, lax.rem(ahead, slots)):
                copy.start()

        slot = lax.rem(step, slots)
        for copy in copies(step, slot):
            copy.wait()
        factor_high, factor_low = halves(factors[slot])
        solved_both = jnp.concatenate(halves(solves[slot]), axis=1)
        total[...] += dot_f32(factor_high, solved_both) + dot_f32(factor_low, solved_both)
        return carry

    lax.fori_loop(0, steps, body, 0)
    fetch_right.wait()
    keep = first_ref[0] == 0
    width = right.shape[1]
    for part in range(PLANES):
        rows = slice(part * 128, part * 128 + 128)
        earlier = total[rows, :width] + total[rows, width:]
        out_ref[part] = (jnp.where(keep, right[rows, :], 0.0) - earlier).T


def in_hbm(*arrays):
    return tuple(pltpu.with_memory_space_constraint(a, pltpu.HBM) for a in arrays)


def earlier_residual(first, factor, solved, right):
    rows, depth = factor.shape
    columns = solved.shape[1]
    tile = next(t for t in (1152, 1024, 768, 512, 256, 128) if depth % t == 0)
    slots = 4
    anywhere = pl.BlockSpec(memory_space=pl.ANY)
    return pl.pallas_call(
        functools.partial(earlier_sums, tile),
        out_shape=jax.ShapeDtypeStruct((PLANES, columns, 128), F32),
        in_specs=[pl.BlockSpec(memory_space=pltpu.SMEM)] + [anywhere] * 3,
        out_specs=pl.BlockSpec(memory_space=pltpu.VMEM),
        scratch_shapes=[
            pltpu.VMEM((slots, rows, tile), F32),
            pltpu.VMEM((slots, tile, columns), F32),
            pltpu.VMEM((rows, columns), F32),
            pltpu.VMEM((rows, 2 * columns), F32),
            pltpu.SemaphoreType.DMA((3, slots)),
        ],
        compiler_params=pltpu.CompilerParams(vmem_limit_bytes=32 << 20),
        cost_estimate=pl.CostEstimate(
            flops=8 * rows * columns * depth, bytes_accessed=4 * (rows + columns) * depth, transcendentals=0
        ),
        name="earlier",
    )(first, *in_hbm(factor, solved, right))


def pack(window_ref, inverse_ref, out_ref, sems):
    z, x = lax.axis_index("z"), lax.axis_index("x")
    copies = [pltpu.make_async_copy(inverse_ref.at[2 * z + x], out_ref.at[0], sems.at[0])]
    for j in range(1, 8):
        copies.append(pltpu.make_async_copy(window_ref.at[lax.rem(2 * z + j, 8)], out_ref.at[j], sems.at[j]))
    for copy in copies:
        copy.start()
    for copy in copies:
        copy.wait()


def place_piece(piece, y, core, x, other, dy, dx, start, outs):
    row_part = 2 * (y + dy - 2 * y * dy) + (core + other - 2 * core * other)
    column = x + dx - 2 * x * dx
    for j in range(piece.shape[0]):
        apart, b = (start + j) // 2, (start + j) % 2
        if apart == 0:
            b = column if b == 0 else 1 - column
        row = pl.multiple_of(b * 256 + row_part * 64, 64)
        where = (pl.ds(row, 64), pl.ds(pl.multiple_of(column * 256, 256), 256))
        for part, value in enumerate(halves(piece[j])):
            outs[apart][(part,) + where] = value


def arrange(spots, kept, *refs):
    count = len(spots)
    pieces, (held, sems) = refs[:count], refs[-2:]
    outs = refs[count + kept : -2]
    y, core, x = (lax.axis_index(a) for a in ("y", "core", "x"))
    copies = [pltpu.make_async_copy(pieces[i], held.at[i], sems.at[i]) for i in range(count)]
    for copy in copies:
        copy.start()
    for i, copy in enumerate(copies):
        copy.wait()
        other, dy, dx, start = spots[i]
        place_piece(held.at[i], y, core, x, other, dy, dx, start, outs)


def arranged(name, spots, pieces, *weights):
    in_vmem = pl.BlockSpec(memory_space=pltpu.VMEM)
    count = len(pieces)
    return pl.pallas_call(
        functools.partial(arrange, spots, len(weights)),
        out_shape=[jax.ShapeDtypeStruct((2, SUPER, SUPER), BF16)] * 4,
        in_specs=[pl.BlockSpec(memory_space=pl.ANY)] * count + [in_vmem] * len(weights),
        out_specs=[in_vmem] * 4,
        scratch_shapes=[pltpu.VMEM((count, *pieces[0].shape), F32), pltpu.SemaphoreType.DMA((count,))],
        input_output_aliases={count + i: i for i in range(len(weights))},
        compiler_params=pltpu.CompilerParams(vmem_limit_bytes=8 << 20),
        name=name,
    )(*pieces, *weights)


def product(left, right):
    return dot_f32(left[0], right[0]) + (dot_f32(left[1], right[0]) + dot_f32(left[0], right[1]))


def both_parts(weight_ref, rows=slice(0, SUPER), columns=slice(0, SUPER)):
    return weight_ref[0, rows, columns], weight_ref[1, rows, columns]


def invert(here_ref, out_ref):
    top, bottom = slice(0, 256), slice(256, 512)
    first, second = both_parts(here_ref, top, top), both_parts(here_ref, bottom, bottom)
    below = halves(product(both_parts(here_ref, bottom, top), first))
    corner = halves(-product(second, below))
    for part in range(2):
        out_ref[part, top, top] = first[part]
        out_ref[part, top, bottom] = jnp.zeros((256, 256), BF16)
        out_ref[part, bottom, top] = corner[part]
        out_ref[part, bottom, bottom] = second[part]


def combine(inverse_ref, near_ref, far_ref, *out_refs):
    inverse = both_parts(inverse_ref)
    for weight_ref, out_ref in zip((near_ref, far_ref), out_refs):
        out_ref[0], out_ref[1] = halves(product(both_parts(weight_ref), inverse))


def apply(value, weight_ref):
    high, low = halves(value)
    count = value.shape[0]
    first = dot_rows(jnp.concatenate([high, low], axis=0), weight_ref[0])
    return first[:count] + first[count:] + dot_rows(high, weight_ref[1])


def chain_first(parts_ref, inverse_ref, near_ref, far_ref, residual_ref, solved_ref, out_ref):
    by_rows = []
    for row_part in range(4):
        terms = [parts_ref[z, row_part, x] for z in range(PLANES) for x in range(2)]
        while len(terms) > 1:
            terms = [terms[i] + terms[i + 1] for i in range(0, len(terms), 2)]
        by_rows.append(terms[0])
    residual = jnp.concatenate([t[:, :64] for t in by_rows] + [t[:, 64:] for t in by_rows], axis=1)
    residual_ref[...] = residual
    solved = apply(residual, inverse_ref)
    solved_ref[...] = solved
    out_ref[0] = apply(solved, near_ref)
    out_ref[1] = apply(solved, far_ref)


def chain_direct(solved_ref, farthest_ref, out_ref, held, sem):
    fetch = pltpu.make_async_copy(farthest_ref, held, sem)
    fetch.start()
    fetch.wait()
    out_ref[...] = apply(solved_ref[...], held)


def chain_middle(residual_ref, received_ref, near_ref, next_ref, out_ref):
    residual = residual_ref[...] - received_ref[0]
    next_ref[...] = residual
    term = apply(residual, near_ref)
    out_ref[0] = received_ref[1] + term if received_ref.shape[0] > 1 else term


def chain_second_direct(residual_ref, far_ref, out_ref):
    out_ref[...] = apply(residual_ref[...], far_ref)


def chain_last(residual_ref, received_ref, direct_ref, second_ref, inverse_ref, out_ref):
    solved = apply(residual_ref[...] - ((received_ref[0] + second_ref[...]) + direct_ref[...]), inverse_ref)
    for row_part in range(4):
        start = row_part * 64
        chunk = jnp.concatenate([solved[:, start : start + 64], solved[:, start + 256 : start + 320]], axis=1)
        for z in range(PLANES):
            for x in range(2):
                out_ref[z, row_part, x] = chunk


def split(first_ref, second_ref, low_ref, high_ref):
    low_ref[...] = first_ref[:4]
    high_ref[...] = second_ref[4:]


def turn(parts_ref, out_ref):
    for part in range(PLANES):
        out_ref[part] = parts_ref[part].T


def call(kernel, name, outs, *args, large=(), scratch=(), flops=None):
    in_vmem = pl.BlockSpec(memory_space=pltpu.VMEM)
    return pl.pallas_call(
        kernel,
        out_shape=[jax.ShapeDtypeStruct(*o) for o in outs],
        in_specs=[in_vmem] * len(args) + [pl.BlockSpec(memory_space=pl.ANY)] * len(large),
        out_specs=[in_vmem] * len(outs),
        scratch_shapes=scratch,
        compiler_params=pltpu.CompilerParams(vmem_limit_bytes=8 << 20),
        cost_estimate=flops and pl.CostEstimate(flops=flops, bytes_accessed=1 << 21, transcendentals=0),
        name=name,
    )(*args, *in_hbm(*large))


def local(right_side, lower_prev, solved_prev, lower_window, inverse_diag):
    blocks, local_rows, columns = right_side.shape
    depth = lower_prev.shape[2]
    swap = functools.partial(lax.ppermute, perm=SWAP)
    message = pl.pallas_call(
        pack,
        out_shape=jax.ShapeDtypeStruct(lower_window.shape, F32),
        in_specs=[pl.BlockSpec(memory_space=pl.ANY)] * 2,
        out_specs=pl.BlockSpec(memory_space=pltpu.VMEM),
        scratch_shapes=[pltpu.SemaphoreType.DMA((8,))],
        compiler_params=pltpu.CompilerParams(vmem_limit_bytes=4 << 20),
        name="pack",
    )(*in_hbm(lower_window, inverse_diag))

    from_x = swap(message, "x")
    from_y = swap(message, "y")
    from_core = swap(message, "core")

    factor = lower_prev.reshape(blocks * local_rows, depth)
    right = right_side.reshape(blocks * local_rows, columns)
    first = (2 * lax.axis_index("z") + lax.axis_index("x")).astype(jnp.int32).reshape(1)
    parts = earlier_residual(first, factor, solved_prev, right)

    parts, from_x, from_y = lax.optimization_barrier((parts, from_x, from_y))
    half = ((4, *lower_window.shape[1:]), F32)
    low, high = call(split, "split", [half] * 2, from_x, from_y)
    corner_low, corner_high = swap(low, "y"), swap(high, "x")
    core_x, core_y = swap(from_x, "core"), swap(from_y, "core")
    parts = lax.all_to_all(parts.reshape(32, RHS_PART, 128), EVERY, 0, 0, tiled=True)
    core_low, core_high = swap(corner_low, "core"), swap(corner_high, "core")
    pieces = (message, from_x, from_y, from_core, core_x, core_y)
    spots = ((0, 0, 0, 0), (0, 0, 1, 0), (0, 1, 0, 0), (1, 0, 0, 0), (1, 0, 1, 0), (1, 1, 0, 0))
    weights = arranged("arrange", spots, in_hbm(*pieces))
    pieces = (corner_low, corner_high, core_low, core_high)
    weights = arranged("arrange_corner", ((0, 1, 1, 0), (0, 1, 1, 4), (1, 1, 1, 0), (1, 1, 1, 4)), pieces, *weights)

    here, near, far, farthest = weights
    weight = ((2, SUPER, SUPER), BF16)
    (inverse,) = call(invert, "invert", [weight], here, flops=6 * 256**3 * 2)

    def vectors(*counts):
        return ((*counts, RHS_PART, SUPER), F32)

    parts = parts.reshape(4, 4, 2, RHS_PART, 128)
    scratch = [pltpu.VMEM((2, SUPER, SUPER), BF16), pltpu.SemaphoreType.DMA]
    outs = [vectors(), vectors(), vectors(2)]
    residual, solved, sent = call(chain_first, "chain_first", outs, parts, inverse, near, far)
    (direct,) = call(
        chain_direct, "chain_direct", [vectors()], solved, large=[farthest], scratch=scratch, flops=6 * 16 * SUPER**2
    )
    direct = lax.ppermute(direct, "z", [(0, 3)])
    combined = call(combine, "combine", [weight] * 2, inverse, near, far, flops=6 * SUPER**3 * 2)
    for step in (1, 2):
        received = lax.ppermute(sent, "z", [(step - 1, step)])
        residual, sent = call(chain_middle, "chain_middle", [vectors(), vectors(1)], residual, received, combined[0])
        if step == 1:
            (second,) = call(
                chain_second_direct, "chain_second_direct", [vectors()], residual, combined[1], flops=6 * 16 * SUPER**2
            )
            second = lax.ppermute(second, "z", [(1, 3)])
    received = lax.ppermute(sent, "z", [(2, 3)])
    chunk = ((4, 4, 2, RHS_PART, 128), F32)
    (chunks,) = call(chain_last, "chain_last", [chunk], residual, received, direct, second, inverse)
    solved = lax.all_to_all(chunks.reshape(32, RHS_PART, 128), EVERY, 0, 0, tiled=True)
    (result,) = call(turn, "turn", [((PLANES, 128, columns), F32)], solved.reshape(PLANES, columns, 128))
    return result.reshape(blocks, local_rows, columns)


def local_any(right_side, lower_prev, solved_prev, lower_window, inverse_diag):
    highest = lax.Precision.HIGHEST
    blocks, local_rows, columns = right_side.shape
    block_rows = inverse_diag.shape[2]
    row_start = lax.axis_index("prow") * local_rows
    solved = jnp.zeros((blocks * block_rows, columns), F32)
    pieces = []
    full_inverse = lax.all_gather(inverse_diag, "prow", axis=1, tiled=True)
    full_window = lax.all_gather(lower_window, "pcol", axis=2, tiled=True)
    dot = functools.partial(jnp.dot, precision=highest, preferred_element_type=F32)
    for row_block in range(blocks):
        window_term = dot(full_window[row_block], solved)
        earlier_here = lax.psum(dot(lower_prev[row_block], solved_prev), "pcol")
        local_residual = right_side[row_block] - (earlier_here + window_term)
        residual = lax.all_gather(local_residual, "prow", axis=0, tiled=True)
        whole_rows = dot(full_inverse[row_block], residual)
        pieces.append(lax.dynamic_slice_in_dim(whole_rows, row_start, local_rows, 0))
        solved = lax.dynamic_update_slice_in_dim(solved, whole_rows, row_block * block_rows, 0)
    return jnp.stack(pieces)


def run(mesh, body, row, column):
    in_specs = (P(None, row, None), P(None, row, column), P(column, None), P(None, row, column), P(None, row, None))
    return jax.shard_map(body, mesh=mesh, in_specs=in_specs, out_specs=P(None, row, None), check_vma=False)


def solution(mesh):
    if (mesh.shape["prow"], mesh.shape["pcol"]) == (4, 8):
        fine = Mesh(mesh.devices.reshape(2, 2, 4, 2), ("y", "core", "z", "x"))
        return run(fine, local, ("y", "core"), ("z", "x"))
    return run(mesh, local_any, "prow", "pcol")
```

```python
import functools

import jax
import jax.numpy as jnp
from jax import lax
from jax.experimental import pallas as pl
from jax.experimental.pallas import tpu as pltpu
from jax.sharding import Mesh, PartitionSpec as P

F32 = jnp.float32
BF16 = jnp.bfloat16
EVERY = ("z", "y", "core", "x")
SWAP = [(0, 1), (1, 0)]
PLANES = 4
RHS_PART = 16
SUPER = 512


def halves(value):
    high = value.astype(BF16)
    low = (value - high.astype(F32)).astype(BF16)
    return high, low


def dot_f32(a, b):
    return jnp.dot(a, b, preferred_element_type=F32)


def dot_rows(a, b):
    return lax.dot_general(a, b, (((1,), (1,)), ((), ())), preferred_element_type=F32)


def earlier_sums(tile, first_ref, factor_ref, solved_ref, right_ref, out_ref, factors, solves, right, total, sems):
    steps = factor_ref.shape[1] // tile
    slots = factors.shape[0]

    def copies(step, slot):
        where = pl.ds(pl.multiple_of(step * tile, 128), tile)
        return (
            pltpu.make_async_copy(factor_ref.at[:, where], factors.at[slot], sems.at[0, slot]),
            pltpu.make_async_copy(solved_ref.at[where, :], solves.at[slot], sems.at[1, slot]),
        )

    for step in range(min(slots - 1, steps)):
        for copy in copies(step, step):
            copy.start()
    fetch_right = pltpu.make_async_copy(right_ref, right, sems.at[2, 0])
    fetch_right.start()
    total[...] = jnp.zeros_like(total)

    def body(step, carry):
        ahead = step + slots - 1

        @pl.when(ahead < steps)
        def _():
            for copy in copies(ahead, lax.rem(ahead, slots)):
                copy.start()

        slot = lax.rem(step, slots)
        for copy in copies(step, slot):
            copy.wait()
        factor_high, factor_low = halves(factors[slot])
        solved_both = jnp.concatenate(halves(solves[slot]), axis=1)
        total[...] += dot_f32(factor_high, solved_both) + dot_f32(factor_low, solved_both)
        return carry

    lax.fori_loop(0, steps, body, 0)
    fetch_right.wait()
    keep = first_ref[0] == 0
    width = right.shape[1]
    for part in range(PLANES):
        rows = slice(part * 128, part * 128 + 128)
        earlier = total[rows, :width] + total[rows, width:]
        out_ref[part] = (jnp.where(keep, right[rows, :], 0.0) - earlier).T


def in_hbm(*arrays):
    return tuple(pltpu.with_memory_space_constraint(a, pltpu.HBM) for a in arrays)


def earlier_residual(first, factor, solved, right):
    rows, depth = factor.shape
    columns = solved.shape[1]
    tile = next(t for t in (1152, 1024, 768, 512, 256, 128) if depth % t == 0)
    slots = 4
    anywhere = pl.BlockSpec(memory_space=pl.ANY)
    return pl.pallas_call(
        functools.partial(earlier_sums, tile),
        out_shape=jax.ShapeDtypeStruct((PLANES, columns, 128), F32),
        in_specs=[pl.BlockSpec(memory_space=pltpu.SMEM)] + [anywhere] * 3,
        out_specs=pl.BlockSpec(memory_space=pltpu.VMEM),
        scratch_shapes=[
            pltpu.VMEM((slots, rows, tile), F32),
            pltpu.VMEM((slots, tile, columns), F32),
            pltpu.VMEM((rows, columns), F32),
            pltpu.VMEM((rows, 2 * columns), F32),
            pltpu.SemaphoreType.DMA((3, slots)),
        ],
        compiler_params=pltpu.CompilerParams(vmem_limit_bytes=32 << 20),
        cost_estimate=pl.CostEstimate(
            flops=8 * rows * columns * depth, bytes_accessed=4 * (rows + columns) * depth, transcendentals=0
        ),
        name="earlier",
    )(first, *in_hbm(factor, solved, right))


def pack(window_ref, inverse_ref, out_ref, sems):
    z, x = lax.axis_index("z"), lax.axis_index("x")
    copies = [pltpu.make_async_copy(inverse_ref.at[2 * z + x], out_ref.at[0], sems.at[0])]
    for j in range(1, 8):
        copies.append(pltpu.make_async_copy(window_ref.at[lax.rem(2 * z + j, 8)], out_ref.at[j], sems.at[j]))
    for copy in copies:
        copy.start()
    for copy in copies:
        copy.wait()


def place_piece(piece, y, core, x, other, dy, dx, start, outs):
    row_part = 2 * (y + dy - 2 * y * dy) + (core + other - 2 * core * other)
    column = x + dx - 2 * x * dx
    for j in range(piece.shape[0]):
        apart, b = (start + j) // 2, (start + j) % 2
        if apart == 0:
            b = column if b == 0 else 1 - column
        row = pl.multiple_of(b * 256 + row_part * 64, 64)
        where = (pl.ds(row, 64), pl.ds(pl.multiple_of(column * 256, 256), 256))
        for part, value in enumerate(halves(piece[j])):
            outs[apart][(part,) + where] = value


def arrange(spots, kept, *refs):
    count = len(spots)
    pieces, (held, sems) = refs[:count], refs[-2:]
    outs = refs[count + kept : -2]
    y, core, x = (lax.axis_index(a) for a in ("y", "core", "x"))
    copies = [pltpu.make_async_copy(pieces[i], held.at[i], sems.at[i]) for i in range(count)]
    for copy in copies:
        copy.start()
    for i, copy in enumerate(copies):
        copy.wait()
        other, dy, dx, start = spots[i]
        place_piece(held.at[i], y, core, x, other, dy, dx, start, outs)


def arranged(name, spots, pieces, *weights):
    in_vmem = pl.BlockSpec(memory_space=pltpu.VMEM)
    count = len(pieces)
    return pl.pallas_call(
        functools.partial(arrange, spots, len(weights)),
        out_shape=[jax.ShapeDtypeStruct((2, SUPER, SUPER), BF16)] * 4,
        in_specs=[pl.BlockSpec(memory_space=pl.ANY)] * count + [in_vmem] * len(weights),
        out_specs=[in_vmem] * 4,
        scratch_shapes=[pltpu.VMEM((count, *pieces[0].shape), F32), pltpu.SemaphoreType.DMA((count,))],
        input_output_aliases={count + i: i for i in range(len(weights))},
        compiler_params=pltpu.CompilerParams(vmem_limit_bytes=8 << 20),
        name=name,
    )(*pieces, *weights)


def product(left, right):
    return dot_f32(left[0], right[0]) + (dot_f32(left[1], right[0]) + dot_f32(left[0], right[1]))


def both_parts(weight_ref, rows=slice(0, SUPER), columns=slice(0, SUPER)):
    return weight_ref[0, rows, columns], weight_ref[1, rows, columns]


def invert(here_ref, out_ref):
    top, bottom = slice(0, 256), slice(256, 512)
    first, second = both_parts(here_ref, top, top), both_parts(here_ref, bottom, bottom)
    below = halves(product(both_parts(here_ref, bottom, top), first))
    corner = halves(-product(second, below))
    for part in range(2):
        out_ref[part, top, top] = first[part]
        out_ref[part, top, bottom] = jnp.zeros((256, 256), BF16)
        out_ref[part, bottom, top] = corner[part]
        out_ref[part, bottom, bottom] = second[part]


def combine(inverse_ref, near_ref, far_ref, *out_refs):
    inverse = both_parts(inverse_ref)
    for weight_ref, out_ref in zip((near_ref, far_ref), out_refs):
        out_ref[0], out_ref[1] = halves(product(both_parts(weight_ref), inverse))


def apply(value, weight_ref):
    high, low = halves(value)
    count = value.shape[0]
    first = dot_rows(jnp.concatenate([high, low], axis=0), weight_ref[0])
    return first[:count] + first[count:] + dot_rows(high, weight_ref[1])


def chain_first(parts_ref, inverse_ref, near_ref, residual_ref, solved_ref, out_ref):
    by_rows = []
    for row_part in range(4):
        terms = [parts_ref[z, row_part, x] for z in range(PLANES) for x in range(2)]
        while len(terms) > 1:
            terms = [terms[i] + terms[i + 1] for i in range(0, len(terms), 2)]
        by_rows.append(terms[0])
    residual = jnp.concatenate([t[:, :64] for t in by_rows] + [t[:, 64:] for t in by_rows], axis=1)
    residual_ref[...] = residual
    solved = apply(residual, inverse_ref)
    solved_ref[...] = solved
    out_ref[0] = apply(solved, near_ref)


def chain_direct(solved_ref, farthest_ref, out_ref, held, sem):
    fetch = pltpu.make_async_copy(farthest_ref, held, sem)
    fetch.start()
    fetch.wait()
    out_ref[...] = apply(solved_ref[...], held)


def chain_middle(residual_ref, received_ref, *refs):
    more_refs, (near_ref, next_ref, out_ref) = refs[:-3], refs[-3:]
    earlier = received_ref[0]
    for more_ref in more_refs:
        earlier += more_ref[...]
    residual = residual_ref[...] - earlier
    next_ref[...] = residual
    out_ref[0] = apply(residual, near_ref)


def chain_second_direct(residual_ref, far_ref, out_ref):
    out_ref[...] = apply(residual_ref[...], far_ref)


def chain_last(residual_ref, received_ref, direct_ref, second_ref, inverse_ref, out_ref):
    solved = apply(residual_ref[...] - ((received_ref[0] + second_ref[...]) + direct_ref[...]), inverse_ref)
    for row_part in range(4):
        start = row_part * 64
        chunk = jnp.concatenate([solved[:, start : start + 64], solved[:, start + 256 : start + 320]], axis=1)
        for z in range(PLANES):
            for x in range(2):
                out_ref[z, row_part, x] = chunk


def split(first_ref, second_ref, low_ref, high_ref):
    low_ref[...] = first_ref[:4]
    high_ref[...] = second_ref[4:]


def turn(parts_ref, out_ref):
    for part in range(PLANES):
        out_ref[part] = parts_ref[part].T


def call(kernel, name, outs, *args, large=(), scratch=(), flops=None):
    in_vmem = pl.BlockSpec(memory_space=pltpu.VMEM)
    return pl.pallas_call(
        kernel,
        out_shape=[jax.ShapeDtypeStruct(*o) for o in outs],
        in_specs=[in_vmem] * len(args) + [pl.BlockSpec(memory_space=pl.ANY)] * len(large),
        out_specs=[in_vmem] * len(outs),
        scratch_shapes=scratch,
        compiler_params=pltpu.CompilerParams(vmem_limit_bytes=8 << 20),
        cost_estimate=flops and pl.CostEstimate(flops=flops, bytes_accessed=1 << 21, transcendentals=0),
        name=name,
    )(*args, *in_hbm(*large))


def local(right_side, lower_prev, solved_prev, lower_window, inverse_diag):
    blocks, local_rows, columns = right_side.shape
    depth = lower_prev.shape[2]
    swap = functools.partial(lax.ppermute, perm=SWAP)
    message = pl.pallas_call(
        pack,
        out_shape=jax.ShapeDtypeStruct(lower_window.shape, F32),
        in_specs=[pl.BlockSpec(memory_space=pl.ANY)] * 2,
        out_specs=pl.BlockSpec(memory_space=pltpu.VMEM),
        scratch_shapes=[pltpu.SemaphoreType.DMA((8,))],
        compiler_params=pltpu.CompilerParams(vmem_limit_bytes=4 << 20),
        name="pack",
    )(*in_hbm(lower_window, inverse_diag))

    from_x = swap(message, "x")
    from_y = swap(message, "y")
    from_core = swap(message, "core")

    factor = lower_prev.reshape(blocks * local_rows, depth)
    right = right_side.reshape(blocks * local_rows, columns)
    first = (2 * lax.axis_index("z") + lax.axis_index("x")).astype(jnp.int32).reshape(1)
    parts = earlier_residual(first, factor, solved_prev, right)

    parts, from_x, from_y = lax.optimization_barrier((parts, from_x, from_y))
    half = ((4, *lower_window.shape[1:]), F32)
    low, high = call(split, "split", [half] * 2, from_x, from_y)
    corner_low, corner_high = swap(low, "y"), swap(high, "x")
    core_x, core_y = swap(from_x, "core"), swap(from_y, "core")
    parts = lax.all_to_all(parts.reshape(32, RHS_PART, 128), EVERY, 0, 0, tiled=True)
    core_low, core_high = swap(corner_low, "core"), swap(corner_high, "core")
    pieces = (message, from_x, from_y, from_core, core_x, core_y)
    spots = ((0, 0, 0, 0), (0, 0, 1, 0), (0, 1, 0, 0), (1, 0, 0, 0), (1, 0, 1, 0), (1, 1, 0, 0))
    weights = arranged("arrange", spots, in_hbm(*pieces))
    pieces = (corner_low, corner_high, core_low, core_high)
    weights = arranged("arrange_corner", ((0, 1, 1, 0), (0, 1, 1, 4), (1, 1, 1, 0), (1, 1, 1, 4)), pieces, *weights)

    here, near, far, farthest = weights
    weight = ((2, SUPER, SUPER), BF16)
    (inverse,) = call(invert, "invert", [weight], here, flops=6 * 256**3 * 2)

    def vectors(*counts):
        return ((*counts, RHS_PART, SUPER), F32)

    parts = parts.reshape(4, 4, 2, RHS_PART, 128)
    scratch = [pltpu.VMEM((2, SUPER, SUPER), BF16), pltpu.SemaphoreType.DMA]
    outs = [vectors(), vectors(), vectors(1)]
    residual, solved, sent = call(chain_first, "chain_first", outs, parts, inverse, near)
    (direct,) = call(
        chain_direct, "chain_direct", [vectors()], solved, large=[farthest], scratch=scratch, flops=6 * 16 * SUPER**2
    )
    direct = lax.ppermute(direct, "z", [(0, 3)])
    (third,) = call(chain_second_direct, "chain_third_direct", [vectors()], solved, far, flops=6 * 16 * SUPER**2)
    third = lax.ppermute(third, "z", [(0, 2)])
    combined = call(combine, "combine", [weight] * 2, inverse, near, far, flops=6 * SUPER**3 * 2)
    for step in (1, 2):
        received = lax.ppermute(sent, "z", [(step - 1, step)])
        residual, sent = call(chain_middle, "chain_middle", [vectors(), vectors(1)], residual, received, *([third] if step == 2 else []), combined[0])
        if step == 1:
            (second,) = call(
                chain_second_direct, "chain_second_direct", [vectors()], residual, combined[1], flops=6 * 16 * SUPER**2
            )
            second = lax.ppermute(second, "z", [(1, 3)])
    received = lax.ppermute(sent, "z", [(2, 3)])
    chunk = ((4, 4, 2, RHS_PART, 128), F32)
    (chunks,) = call(chain_last, "chain_last", [chunk], residual, received, direct, second, inverse)
    solved = lax.all_to_all(chunks.reshape(32, RHS_PART, 128), EVERY, 0, 0, tiled=True)
    (result,) = call(turn, "turn", [((PLANES, 128, columns), F32)], solved.reshape(PLANES, columns, 128))
    return result.reshape(blocks, local_rows, columns)


def local_any(right_side, lower_prev, solved_prev, lower_window, inverse_diag):
    highest = lax.Precision.HIGHEST
    blocks, local_rows, columns = right_side.shape
    block_rows = inverse_diag.shape[2]
    row_start = lax.axis_index("prow") * local_rows
    solved = jnp.zeros((blocks * block_rows, columns), F32)
    pieces = []
    full_inverse = lax.all_gather(inverse_diag, "prow", axis=1, tiled=True)
    full_window = lax.all_gather(lower_window, "pcol", axis=2, tiled=True)
    dot = functools.partial(jnp.dot, precision=highest, preferred_element_type=F32)
    for row_block in range(blocks):
        window_term = dot(full_window[row_block], solved)
        earlier_here = lax.psum(dot(lower_prev[row_block], solved_prev), "pcol")
        local_residual = right_side[row_block] - (earlier_here + window_term)
        residual = lax.all_gather(local_residual, "prow", axis=0, tiled=True)
        whole_rows = dot(full_inverse[row_block], residual)
        pieces.append(lax.dynamic_slice_in_dim(whole_rows, row_start, local_rows, 0))
        solved = lax.dynamic_update_slice_in_dim(solved, whole_rows, row_block * block_rows, 0)
    return jnp.stack(pieces)


def run(mesh, body, row, column):
    in_specs = (P(None, row, None), P(None, row, column), P(column, None), P(None, row, column), P(None, row, None))
    return jax.shard_map(body, mesh=mesh, in_specs=in_specs, out_specs=P(None, row, None), check_vma=False)


def solution(mesh):
    if (mesh.shape["prow"], mesh.shape["pcol"]) == (4, 8):
        fine = Mesh(mesh.devices.reshape(2, 2, 4, 2), ("y", "core", "z", "x"))
        return run(fine, local, ("y", "core"), ("z", "x"))
    return run(mesh, local_any, "prow", "pcol")
```
